32 devices in a mesh: layer: 4 (over x, core), row: 2 (over y), col: 4 (over z).
Axes of the slice: x: 2, y: 2, z: 4, core: 2. Of those that a mesh axis runs over, the one named last changes fastest.
Arguments:
- schur_window: float32 [4, 2, 256, 2, 4, 256], P(None, 'row', None, None, 'col'), may hold values from -8 to 24, as said below
Outputs:
- factored: float32 [4, 2, 256, 2, 4, 256], P(None, 'row', 'layer', None, 'col')
The draws below stay inside these ranges and needn't reach their ends.
Inputs may be any that keep to these rules, and one draw needn't show every extreme that they name: `schur_window`: the leading 2048 columns of a symmetric positive definite matrix: its leading 2048 x 2048 block is symmetric and positive definite.
All inputs are finite; a program needn't handle non-finite values.
Results may differ from the reference program's by a relative error of at most 0.0001.
Values sent between devices are 32-bit elements; how exact they have to be, the bound alone decides.
A program may use at most 64 MiB of HBM per device.

```python
import math
import jax
import jax.numpy as jnp
from jax import lax

PANEL = 256
PANELS = 2
ROW_BLOCKS = 4
COL_BLOCKS = 2
ROWS = 2048
COLS = 2048
N_ROW = 2
N_COL = 4


def draw_schur_window(key, part):
    row_total = ROW_BLOCKS * N_ROW * PANEL
    col_total = COL_BLOCKS * N_COL * PANEL
    rank_total = PANELS * PANEL
    noise_key, factor_key, diagonal_key = jax.random.split(key, 3)
    rough_part = jax.random.normal(noise_key, (row_total, col_total), jnp.float32)
    factor_draw = jax.random.normal(factor_key, (row_total, rank_total), jnp.float32)
    upper_noise = rough_part[:col_total]
    symmetric_top = (upper_noise + upper_noise.T) * 0.7071067811865476
    rough_part = jnp.concatenate([symmetric_top, rough_part[col_total:]], axis=0) * (0.25 / math.sqrt(col_total))
    coupling = jnp.dot(factor_draw, factor_draw[:col_total].T, precision=lax.Precision.HIGHEST) * (4.0 / rank_total)
    diagonal = jax.random.uniform(diagonal_key, (col_total,), jnp.float32, 2.0, 4.0)
    positions = jnp.arange(col_total, dtype=jnp.int32)
    matrix_draw = (rough_part + coupling).at[positions, positions].add(diagonal)
    return matrix_draw.reshape(ROW_BLOCKS, N_ROW, PANEL, COL_BLOCKS, N_COL, PANEL)


def setup_inputs(seed: int = 0) -> dict:
    streams_of = jax.random.split(jax.random.key(seed), 2)
    return {
        "schur_window": draw_schur_window(jax.random.fold_in(streams_of[1], 71), 0),
    }


def reference(schur_window):
    matrix = schur_window.reshape(ROWS, COLS)
    row_block = (jnp.arange(ROWS, dtype=jnp.int32) // PANEL)[:, None]
    for panel_index in range(PANELS):
        block_start = panel_index * PANEL
        block_end = block_start + PANEL
        factor = jnp.linalg.cholesky(matrix[block_start:block_end, block_start:block_end])
        solved = jax.scipy.linalg.solve_triangular(factor, matrix[:, block_start:block_end].T, lower=True).T
        column = jnp.where(row_block > panel_index, solved, jnp.zeros_like(solved))
        column = column.at[block_start:block_end].set(factor)
        update = jnp.dot(column[block_end:].astype(jnp.float32), column[block_end:COLS].T.astype(jnp.float32), precision=lax.Precision.HIGHEST, preferred_element_type=jnp.float32)
        matrix = matrix.at[block_end:, block_end:].add(-update)
        matrix = matrix.at[:, block_start:block_end].set(column)
        matrix = matrix.at[block_start:block_end, block_end:].set(jnp.zeros((PANEL, COLS - block_end), jnp.float32))
    return matrix.reshape(schur_window.shape)
```

```python
import functools

import jax
import jax.numpy as jnp
from jax import lax
from jax.experimental import pallas as pl
from jax.experimental.pallas import tpu as pltpu
from jax.sharding import PartitionSpec as P

PANELS = 2
SUB = 8
STEP = 32
SPAN = 2
PIECES = ((0, 0, 0, 0, 0), (0, 0, 0, 1, None), (1, 0, 1, None, None), (1, 1, 2, None, None))


def dot(a, b, lhs, rhs):
    return lax.dot_general(
        a, b, (((lhs,), (rhs,)), ((), ())),
        precision=lax.Precision.HIGHEST, preferred_element_type=jnp.float32,
    )


def matmul(a, b):
    return dot(a, b, 1, 0)


def matmul_t(a, b):
    return dot(a, b, 1, 1)


def update(a, b, rhs):
    a0, b0 = a.astype(jnp.bfloat16), b.astype(jnp.bfloat16)
    a1 = (a - a0.astype(jnp.float32)).astype(jnp.bfloat16)
    b1 = (b - b0.astype(jnp.float32)).astype(jnp.bfloat16)

    def product(x, y):
        return lax.dot_general(x, y, (((1,), (rhs,)), ((), ())), preferred_element_type=jnp.float32)

    return product(a0, b0) + (product(a0, b1) + product(a1, b0))


def spread(tile, start, count):
    size, lanes = tile.shape
    return [
        jnp.broadcast_to(tile[m // SUB * SUB :, start + m : start + m + 1], (size - m // SUB * SUB, lanes))
        for m in range(count)
    ]


def invert(aug, width, hook):
    sub = lax.broadcasted_iota(jnp.int32, (SUB, width), 0)
    lane = lax.broadcasted_iota(jnp.int32, (STEP, width), 1)
    row_in = lax.broadcasted_iota(jnp.int32, (STEP, width), 0)
    lane_below = lax.broadcasted_iota(jnp.int32, (width - STEP, width), 1)
    eye = jnp.where(lane == row_in, 1.0, 0.0).astype(jnp.float32)
    groups = STEP // SUB

    def step(s, carry):
        if hook is not None:
            hook(s)
        rest = aug[:STEP, :]
        below_rows = pltpu.roll(jnp.where(lane_below < STEP, 0.0, aug[STEP:, :]), width - STEP, 1)
        keep = row_in < STEP + s
        finished = []
        for g in range(groups):
            if g % SPAN == 0:
                column = spread(rest, g * SUB, SPAN * SUB)
                own = (lane >= g * SUB) & (lane < (g + SPAN) * SUB)
                rest = jnp.where(own[g * SUB :], eye[g * SUB :], rest)
                column = [jnp.where(keep[: c.shape[0]], c, 0.0) for c in column]
            rows = [jnp.broadcast_to(rest[j : j + 1, :], (SUB, width)) for j in range(SUB)]
            entry = [
                [jnp.broadcast_to(column[k][j : j + 1, :], (SUB, width)) if k >= j else None for k in range(SUB)]
                for j in range(SUB)
            ]
            done = jnp.zeros((SUB, width), jnp.float32)
            scales, lows = [], []
            for j in range(SUB):
                scale = lax.rsqrt(entry[j][j])
                rows[j] = rows[j] * scale
                done = jnp.where(sub == j, rows[j], done)
                low = [entry[j][k] * scale if k > j else None for k in range(SUB)]
                for k in range(j + 1, SUB):
                    for m in range(k, SUB):
                        entry[k][m] = entry[k][m] - low[k] * low[m]
                    rows[k] = rows[k] - low[k] * rows[j]
                scales.append(scale)
                lows.append(low)
            finished.append(done)
            after = groups - 1 - g
            if not after:
                break

            def tall(value):
                return jnp.concatenate([value] * after, axis=0) if after > 1 else value

            lower = []
            for j in range(SUB):
                c = column[j][SUB:, :]
                for i in range(j):
                    c = c - lower[i] * tall(lows[i][j])
                lower.append(c * tall(scales[j]))
            later = []
            for m in range(SUB, len(column)) if g % SPAN < SPAN - 1 else ():
                c = column[m]
                for j in range(SUB):
                    c = c - lower[j][m // SUB * SUB - SUB :, :] * lower[j][m - SUB : m - SUB + 1, :]
                later.append(c)
            rest = rest[SUB:, :]
            for j in range(SUB):
                rest = rest - lower[j] * tall(rows[j])
            column = later
        done = jnp.concatenate(finished, axis=0)
        done = jnp.where((lane < STEP) & (lane >= (row_in // (SPAN * SUB) + 1) * (SPAN * SUB)), 0.0, done)
        across = jnp.where((lane >= STEP) & (lane < width - s * STEP), done, 0.0)
        turned = pltpu.roll(done, width - STEP, 1)
        aug[: width - STEP, :] = below_rows - matmul(across.T[STEP:], turned)
        aug[width - STEP :, :] = turned
        return carry

    lax.fori_loop(0, width // STEP, step, 0)


def kernel(
    sizes, window, out, diag, across, panel, share, staged, aug, inverse, cross, rest, left,
    diag_send, diag_recv, pass_send, pass_recv, across_send, across_recv, panel_send, panel_recv, share_sem, out_sem,
):
    layers, grid_rows, grid_cols, row_blocks, col_blocks, width = sizes
    rows_here = width // layers
    half = width // 2
    split = 2 if grid_rows % 2 == 0 else 1
    skip = 1 if grid_rows <= PANELS else 0
    me_layer, me_row, me_col = lax.axis_index("layer"), lax.axis_index("row"), lax.axis_index("col")
    mine = lax.rem(me_row, split)

    def at(layer, row, col):
        return (lax.rem(me_layer + layer, layers), lax.rem(me_row + row, grid_rows), lax.rem(me_col + col, grid_cols))

    def mate(layer, part):
        return (lax.rem(me_layer + layer, layers), me_row - mine + lax.rem(mine + part, split), me_col)

    def remote(src, dst, send, recv, target):
        return pltpu.make_async_remote_copy(
            src_ref=src, dst_ref=dst, send_sem=send, recv_sem=recv, device_id=target,
            device_id_type=pl.DeviceIdType.MESH,
        )

    def wait(ref, sem):
        pltpu.make_async_copy(ref, ref, sem).wait()

    here = pl.ds(pl.multiple_of(me_layer * rows_here, rows_here), rows_here)
    share_copies = [
        pltpu.make_async_copy(window.at[:, 0, here, slot, 0, :], share.at[slot], share_sem.at[slot])
        for slot in range(col_blocks)
    ]

    peers = [(row, col) for col in reversed(range(grid_cols)) for row in range(grid_rows) if row or col]
    mates = [(layer, part) for layer in range(layers) for part in range(split) if layer or part]
    barrier = pltpu.get_barrier_semaphore()
    for row, col in peers:
        pl.semaphore_signal(barrier, inc=1, device_id=at(0, row, col), device_id_type=pl.DeviceIdType.MESH)
    for layer, part in mates:
        if layer:
            pl.semaphore_signal(barrier, inc=1, device_id=mate(layer, part), device_id_type=pl.DeviceIdType.MESH)
    diag[0, :half, half:] = jnp.zeros((half, width - half), jnp.float32)
    pl.semaphore_wait(barrier, len(peers) + len(mates) - split + 1)

    def extent(p):
        _, _, slot, lower, side = PIECES[p]
        first, count = (0, width) if lower is None else (lower * half, half)
        return slot, first, count, pl.ds(0, width if side is None else half)

    def part_rows(p, part):
        _, first, count, _ = extent(p)
        size = count // (layers * split)
        return pl.ds(pl.multiple_of(first + (me_layer * split + part) * size, size), size)

    def diag_src(p, part):
        return window.at[0, 0, part_rows(p, part), 0, 0, extent(p)[3]]

    def diag_dst(p, part):
        return diag.at[extent(p)[0], part_rows(p, part), extent(p)[3]]

    def some(p, parts):
        slot, first, count, columns = extent(p)
        return diag.at[slot, pl.ds(first, parts * (count // (layers * split))), columns]

    def diag_copy(p, row, col):
        part = lax.rem(lax.rem(me_row + row, grid_rows), split)
        return remote(diag_src(p, part), diag_dst(p, part), diag_send.at[p, col], diag_recv.at[p], at(0, row, col))

    def diag_local(p):
        return pltpu.make_async_copy(diag_src(p, mine), diag_dst(p, mine), diag_recv.at[p])

    owners = [(me_row == piece[0]) & (me_col == piece[1]) for piece in PIECES]

    def diag_out(p):
        @pl.when(owners[p])
        def _():
            for row, col in peers:
                diag_copy(p, row, col).start()
            diag_local(p).start()

    def diag_pass(p):
        wait(diag_dst(p, mine), diag_recv.at[p])
        for layer, part in mates:
            remote(diag_dst(p, mine), diag_dst(p, mine), pass_send.at[p], pass_recv.at[p], mate(layer, part)).start()

    def diag_arrived(p):
        wait(some(p, len(mates)), pass_recv.at[p])

    def panel_src(i):
        return window.at[i, 0, here, 0, 0, :]

    def panel_hop(k, i, src, way):
        return remote(src, panel.at[k, i], panel_send.at[k, 0 if way < 0 else 1], panel_recv.at[k, i], (me_layer, me_row, me_col + way))

    chunks = range(skip, row_blocks)

    def up(k):
        return (me_col >= k) & (me_col < grid_cols - 1)

    def down(k):
        return (me_col <= k) & (me_col > 0)

    def panel_out(k, i, src):
        @pl.when(up(k))
        def _():
            panel_hop(k, i, src, 1).start()

        if k:
            @pl.when(down(k))
            def _():
                panel_hop(k, i, src, -1).start()

    def panel_begin():
        for k in range(PANELS):
            @pl.when(me_col == k)
            def _(k=k):
                for i in chunks:
                    panel_out(k, i, panel_src(i))
                    pltpu.make_async_copy(panel_src(i), panel.at[k, i], panel_recv.at[k, i]).start()

    def panel_next(k, i, distance):
        @pl.when(jnp.abs(me_col - k) == distance)
        def _():
            wait(panel.at[k, i], panel_recv.at[k, i])
            if distance:
                panel_out(k, i, panel.at[k, i])

    def across_begin():
        for k in range(PANELS):
            @pl.when(me_row == k)
            def _(k=k):
                for slot in range(col_blocks):
                    for n in range(1, grid_rows):
                        remote(
                            window.at[0, 0, :, slot, 0, :], across.at[k, slot], across_send.at[k, slot],
                            across_recv.at[k, slot], at(0, n, 0),
                        ).start()
                    pltpu.make_async_copy(window.at[0, 0, :, slot, 0, :], across.at[k, slot], across_recv.at[k, slot]).start()

    steps = half // STEP
    plan = [[] for _ in range(4 * steps)]
    plan[1].append(functools.partial(diag_pass, 1))
    plan[2].append(functools.partial(diag_pass, 2))
    plan[3].append(functools.partial(diag_pass, 3))
    plan[3].append(panel_begin)
    plan[2].append(across_begin)
    final = []
    for distance in range(grid_cols):
        for i in chunks:
            for k in range(PANELS):
                when = 4 + 4 * distance + 2 * (i - skip) if distance else 4 * steps
                (plan[when] if when < 4 * steps else final).append(functools.partial(panel_next, k, i, distance))

    def hook(b):
        def run(s):
            for t in range(steps):
                if plan[b * steps + t]:
                    @pl.when(s == t)
                    def _(t=t):
                        for action in plan[b * steps + t]:
                            action()
        return run

    for p in range(len(PIECES)):
        diag_out(p)
    for copy in share_copies:
        copy.start()
    diag_pass(0)
    diag_arrived(0)

    def inverted(b, value):
        aug[...] = value
        invert(aug, half, hook(b))
        return aug[...]

    def joined(k, first, second, below):
        inverse[k, :half, :half] = first
        inverse[k, :half, half:] = jnp.zeros((half, half), jnp.float32)
        inverse[k, half:, half:] = second
        inverse[k, half:, :half] = -matmul(second, matmul(below, first))

    inv0 = inverted(0, diag[0, :half, :half])
    inverse[0, :half, :half] = inv0
    diag_arrived(1)
    below0 = matmul_t(diag[0, half:, :half], inv0)
    cross[:half, :half] = below0
    inv1 = inverted(1, diag[0, half:, half:] - matmul_t(below0, below0))
    diag_arrived(2)
    below0, inv0 = cross[:half, :half], inverse[0, :half, :half]
    cross0 = matmul_t(diag[1, :, :half], inv0)
    cross1 = matmul_t(diag[1, :, half:] - matmul_t(cross0, below0), inv1)
    cross[:, :half] = cross0
    cross[:, half:] = cross1
    joined(0, inv0, inv1, below0)
    diag_arrived(3)
    rest[...] = diag[2] - matmul_t(cross0, cross0) - matmul_t(cross1, cross1)
    inv2 = inverted(2, rest[:half, :half])
    inverse[1, :half, :half] = inv2
    below1 = matmul_t(rest[half:, :half], inv2)
    left[0, :half, :half] = below1
    inv3 = inverted(3, rest[half:, half:] - matmul_t(below1, below1))
    joined(1, inverse[1, :half, :half], inv3, left[0, :half, :half])

    for action in final:
        action()
    kept = (row_blocks - skip) * rows_here
    left[0, : kept] = matmul_t(panel[0, skip:].reshape(kept, width), inverse[0])
    left[1, : kept] = matmul_t(panel[1, skip:].reshape(kept, width) - update(left[0, :kept], cross[...], 1), inverse[1])
    row = lax.broadcasted_iota(jnp.int32, (rows_here, width), 0) + me_layer * rows_here
    lower = row >= lax.broadcasted_iota(jnp.int32, (rows_here, width), 1)
    factor0 = jnp.where(lower, matmul_t(diag[0, here, :], inverse[0]), 0.0)
    factor1 = jnp.where(lower, matmul_t(rest[here, :], inverse[1]), 0.0)
    plain0 = cross[here, :] if skip else left[0, :rows_here]
    plain1 = factor1 if skip else left[1, :rows_here]
    first0 = jnp.where(me_row == 0, factor0, plain0)
    first1 = jnp.where(me_row == 0, 0.0, jnp.where(me_row == 1, factor1, plain1))

    def out_copy(slot):
        return pltpu.make_async_copy(staged.at[slot], out.at[:, 0, :, slot, 0, :], out_sem.at[slot])

    for slot in range(col_blocks):
        for k in range(PANELS):
            wait(across.at[k, slot], across_recv.at[k, slot])
        share_copies[slot].wait()
        right0 = matmul(inverse[0], across[0, slot])
        right1 = matmul(inverse[1], across[1, slot] - update(cross[...], right0, 0))
        number = slot * grid_cols + me_col
        updated = share[slot, skip:].reshape(kept, width)
        updated -= update(left[0, :kept], right0, 0) + update(left[1, :kept], right1, 0)
        value = jnp.where(number == 0, left[0, :kept], jnp.where(number == 1, left[1, :kept], updated))
        staged[slot, skip:] = value.reshape(row_blocks - skip, rows_here, width)
        plain = 0.0 if skip else jnp.where(me_row < PANELS, 0.0, updated[:rows_here])
        staged[slot, 0] = jnp.where(number == 0, first0, jnp.where(number == 1, first1, plain))
        out_copy(slot).start()

    for p in range(len(PIECES)):
        @pl.when(owners[p])
        def _(p=p):
            for col in range(grid_cols):
                wait(some(p, grid_rows if col else grid_rows - 1), diag_send.at[p, col])

        wait(some(p, len(mates)), pass_send.at[p])
    for k in range(PANELS):
        @pl.when(up(k))
        def _(k=k):
            wait(panel.at[k, skip:], panel_send.at[k, 1])

        if k:
            @pl.when(down(k))
            def _(k=k):
                wait(panel.at[k, skip:], panel_send.at[k, 0])

        @pl.when(me_row == k)
        def _(k=k):
            for slot in range(col_blocks):
                for n in range(1, grid_rows):
                    wait(across.at[k, slot], across_send.at[k, slot])
    for slot in range(col_blocks):
        out_copy(slot).wait()


def local(sizes, schur_window):
    layers, grid_rows, grid_cols, row_blocks, col_blocks, width = sizes
    rows_here = width // layers
    anywhere = pl.BlockSpec(memory_space=pl.ANY)
    dma = pltpu.SemaphoreType.DMA
    pieces, diagonals, half = len(PIECES), len({p[2] for p in PIECES}), width // 2
    f32 = jnp.float32
    return pl.pallas_call(
        functools.partial(kernel, sizes),
        out_shape=jax.ShapeDtypeStruct((row_blocks, 1, rows_here, col_blocks, 1, width), f32),
        in_specs=[anywhere],
        out_specs=anywhere,
        scratch_shapes=[
            pltpu.VMEM((diagonals, width, width), f32),
            pltpu.VMEM((PANELS, col_blocks, width, width), f32),
            pltpu.VMEM((PANELS, row_blocks, rows_here, width), f32),
            pltpu.VMEM((col_blocks, row_blocks, rows_here, width), f32),
            pltpu.VMEM((col_blocks, row_blocks, rows_here, width), f32),
            pltpu.VMEM((half, half), f32),
            pltpu.VMEM((PANELS, width, width), f32),
            pltpu.VMEM((width, width), f32),
            pltpu.VMEM((width, width), f32),
            pltpu.VMEM((PANELS, row_blocks * rows_here, width), f32),
            dma((pieces, grid_cols)),
            dma((pieces,)),
            dma((pieces,)),
            dma((pieces,)),
            dma((PANELS, col_blocks)),
            dma((PANELS, col_blocks)),
            dma((PANELS, 2)),
            dma((PANELS, row_blocks)),
            dma((col_blocks,)),
            dma((col_blocks,)),
        ],
        compiler_params=pltpu.CompilerParams(collective_id=0, has_side_effects=True),
        name="window",
    )(schur_window)


def solution(mesh):
    def body(schur_window):
        row_blocks, _, width, col_blocks, _, _ = schur_window.shape
        sizes = (mesh.shape["layer"], mesh.shape["row"], mesh.shape["col"], row_blocks, col_blocks, width)
        return local(sizes, schur_window)

    return jax.shard_map(
        body,
        mesh=mesh,
        in_specs=(P(None, "row", None, None, "col", None),),
        out_specs=P(None, "row", "layer", None, "col", None),
        check_vma=False,
    )
```

```python
import functools

import jax
import jax.numpy as jnp
from jax import lax
from jax.experimental import pallas as pl
from jax.experimental.pallas import tpu as pltpu
from jax.sharding import PartitionSpec as P

PANELS = 2
SUB = 8
STEP = 32
SPAN = 2
SHARED = (2, 3)
PIECES = ((0, 0, 0, 0, 0), (0, 0, 0, 1, None), (1, 0, 1, None, None), (1, 1, 2, None, None))


def dot(a, b, lhs, rhs):
    return lax.dot_general(
        a, b, (((lhs,), (rhs,)), ((), ())),
        precision=lax.Precision.HIGHEST, preferred_element_type=jnp.float32,
    )


def matmul(a, b):
    return dot(a, b, 1, 0)


def matmul_t(a, b):
    return dot(a, b, 1, 1)


def update(a, b, rhs):
    a0, b0 = a.astype(jnp.bfloat16), b.astype(jnp.bfloat16)
    a1 = (a - a0.astype(jnp.float32)).astype(jnp.bfloat16)
    b1 = (b - b0.astype(jnp.float32)).astype(jnp.bfloat16)

    def product(x, y):
        return lax.dot_general(x, y, (((1,), (rhs,)), ((), ())), preferred_element_type=jnp.float32)

    return product(a0, b0) + (product(a0, b1) + product(a1, b0))


def spread(tile, start, count):
    size, lanes = tile.shape
    return [
        jnp.broadcast_to(tile[m // SUB * SUB :, start + m : start + m + 1], (size - m // SUB * SUB, lanes))
        for m in range(count)
    ]


def invert(aug, width, hook):
    sub = lax.broadcasted_iota(jnp.int32, (SUB, width), 0)
    lane = lax.broadcasted_iota(jnp.int32, (STEP, width), 1)
    row_in = lax.broadcasted_iota(jnp.int32, (STEP, width), 0)
    lane_below = lax.broadcasted_iota(jnp.int32, (width - STEP, width), 1)
    eye = jnp.where(lane == row_in, 1.0, 0.0).astype(jnp.float32)
    groups = STEP // SUB

    def step(s, carry):
        if hook is not None:
            hook(s)
        rest = aug[:STEP, :]
        below_rows = pltpu.roll(jnp.where(lane_below < STEP, 0.0, aug[STEP:, :]), width - STEP, 1)
        keep = row_in < STEP + s
        finished = []
        for g in range(groups):
            if g % SPAN == 0:
                column = spread(rest, g * SUB, SPAN * SUB)
                own = (lane >= g * SUB) & (lane < (g + SPAN) * SUB)
                rest = jnp.where(own[g * SUB :], eye[g * SUB :], rest)
                column = [jnp.where(keep[: c.shape[0]], c, 0.0) for c in column]
            rows = [jnp.broadcast_to(rest[j : j + 1, :], (SUB, width)) for j in range(SUB)]
            entry = [
                [jnp.broadcast_to(column[k][j : j + 1, :], (SUB, width)) if k >= j else None for k in range(SUB)]
                for j in range(SUB)
            ]
            done = jnp.zeros((SUB, width), jnp.float32)
            scales, lows = [], []
            for j in range(SUB):
                scale = lax.rsqrt(entry[j][j])
                rows[j] = rows[j] * scale
                done = jnp.where(sub == j, rows[j], done)
                low = [entry[j][k] * scale if k > j else None for k in range(SUB)]
                for k in range(j + 1, SUB):
                    for m in range(k, SUB):
                        entry[k][m] = entry[k][m] - low[k] * low[m]
                    rows[k] = rows[k] - low[k] * rows[j]
                scales.append(scale)
                lows.append(low)
            finished.append(done)
            after = groups - 1 - g
            if not after:
                break

            def tall(value):
                return jnp.concatenate([value] * after, axis=0) if after > 1 else value

            lower = []
            for j in range(SUB):
                c = column[j][SUB:, :]
                for i in range(j):
                    c = c - lower[i] * tall(lows[i][j])
                lower.append(c * tall(scales[j]))
            later = []
            for m in range(SUB, len(column)) if g % SPAN < SPAN - 1 else ():
                c = column[m]
                for j in range(SUB):
                    c = c - lower[j][m // SUB * SUB - SUB :, :] * lower[j][m - SUB : m - SUB + 1, :]
                later.append(c)
            rest = rest[SUB:, :]
            for j in range(SUB):
                rest = rest - lower[j] * tall(rows[j])
            column = later
        done = jnp.concatenate(finished, axis=0)
        done = jnp.where((lane < STEP) & (lane >= (row_in // (SPAN * SUB) + 1) * (SPAN * SUB)), 0.0, done)
        across = jnp.where((lane >= STEP) & (lane < width - s * STEP), done, 0.0)
        turned = pltpu.roll(done, width - STEP, 1)
        aug[: width - STEP, :] = below_rows - matmul(across.T[STEP:], turned)
        aug[width - STEP :, :] = turned
        return carry

    lax.fori_loop(0, width // STEP, step, 0)


def kernel(
    sizes, window, out, diag, across, panel, share, staged, aug, inverse, cross, rest, left,
    diag_send, diag_recv, pass_send, pass_recv, near_send, near_recv, across_send, across_recv, half_send, half_recv, panel_send,
    panel_recv, share_sem, out_sem,
):
    layers, grid_rows, grid_cols, row_blocks, col_blocks, width = sizes
    rows_here = width // layers
    half = width // 2
    split = 2 if grid_rows % 2 == 0 else 1
    skip = 1 if grid_rows <= PANELS else 0
    me_layer, me_row, me_col = lax.axis_index("layer"), lax.axis_index("row"), lax.axis_index("col")
    mine = lax.rem(me_row, split)
    pair = 2 if layers % 2 == 0 else 1
    odd = lax.rem(me_layer, pair)
    twin = (me_layer + 1 - 2 * odd, me_row, me_col)

    def at(layer, row, col):
        return (lax.rem(me_layer + layer, layers), lax.rem(me_row + row, grid_rows), lax.rem(me_col + col, grid_cols))

    def mate(layer, part):
        return (lax.rem(me_layer + layer, layers), me_row - mine + lax.rem(mine + part, split), me_col)

    def remote(src, dst, send, recv, target):
        return pltpu.make_async_remote_copy(
            src_ref=src, dst_ref=dst, send_sem=send, recv_sem=recv, device_id=target,
            device_id_type=pl.DeviceIdType.MESH,
        )

    def wait(ref, sem):
        pltpu.make_async_copy(ref, ref, sem).wait()

    here = pl.ds(pl.multiple_of(me_layer * rows_here, rows_here), rows_here)
    share_copies = [
        pltpu.make_async_copy(window.at[:, 0, here, slot, 0, :], share.at[slot], share_sem.at[slot])
        for slot in range(col_blocks)
    ]

    peers = [(row, col) for col in reversed(range(grid_cols)) for row in range(grid_rows) if row or col]
    mates = [(layer, part) for layer in range(layers) for part in range(split) if layer or part]
    barrier = pltpu.get_barrier_semaphore()
    for row, col in peers:
        pl.semaphore_signal(barrier, inc=1, device_id=at(0, row, col), device_id_type=pl.DeviceIdType.MESH)
    for layer, part in mates:
        if layer:
            pl.semaphore_signal(barrier, inc=1, device_id=mate(layer, part), device_id_type=pl.DeviceIdType.MESH)
    diag[0, :half, half:] = jnp.zeros((half, width - half), jnp.float32)
    pl.semaphore_wait(barrier, len(peers) + len(mates) - split + 1)

    def extent(p):
        _, _, slot, lower, side = PIECES[p]
        first, count = (0, width) if lower is None else (lower * half, half)
        return slot, first, count, pl.ds(0, width if side is None else half)

    def part_rows(p, part):
        _, first, count, _ = extent(p)
        size = count // (layers * split)
        return pl.ds(pl.multiple_of(first + (me_layer * split + part) * size, size), size)

    def diag_src(p, part):
        return window.at[0, 0, part_rows(p, part), 0, 0, extent(p)[3]]

    def diag_dst(p, part):
        return diag.at[extent(p)[0], part_rows(p, part), extent(p)[3]]

    def some(p, parts):
        slot, first, count, columns = extent(p)
        return diag.at[slot, pl.ds(first, parts * (count // (layers * split))), columns]

    def diag_copy(p, row, col):
        part = lax.rem(lax.rem(me_row + row, grid_rows), split)
        return remote(diag_src(p, part), diag_dst(p, part), diag_send.at[p, col], diag_recv.at[p], at(0, row, col))

    def diag_local(p):
        return pltpu.make_async_copy(diag_src(p, mine), diag_dst(p, mine), diag_recv.at[p])

    owners = [(me_row == piece[0]) & (me_col == piece[1]) for piece in PIECES]

    def diag_out(p):
        @pl.when(owners[p])
        def _():
            for row, col in peers:
                diag_copy(p, row, col).start()
            diag_local(p).start()

    def targets(p):
        return [m for m in mates if p not in SHARED or pair == 1 or m[0] % pair == 0]

    def stripe_rows(p, layer):
        _, first, count, _ = extent(p)
        size = count // layers
        return pl.ds(pl.multiple_of(first + lax.rem(me_layer + layer, layers) * size, size), size)

    def shared(p):
        return p in SHARED and pair > 1

    def diag_pass(p):
        wait(diag_dst(p, mine), diag_recv.at[p])
        for layer, part in targets(p):
            remote(diag_dst(p, mine), diag_dst(p, mine), pass_send.at[p], pass_recv.at[p], mate(layer, part)).start()

    def diag_near(p):
        if shared(p):
            wait(some(p, len(targets(p))), pass_recv.at[p])
            for layer in range(0, layers, pair):
                part = diag.at[extent(p)[0], stripe_rows(p, layer), extent(p)[3]]
                remote(part, part, near_send.at[p], near_recv.at[p], twin).start()

    def diag_arrived(p):
        if shared(p):
            wait(some(p, layers * split // pair), near_recv.at[p])
        else:
            wait(some(p, len(mates)), pass_recv.at[p])

    def panel_src(i):
        return window.at[i, 0, here, 0, 0, :]

    def panel_hop(k, i, src, way):
        return remote(src, panel.at[k, i], panel_send.at[k, 0 if way < 0 else 1], panel_recv.at[k, i], (me_layer, me_row, me_col + way))

    chunks = range(skip, row_blocks)

    def up(k):
        return (me_col >= k) & (me_col < grid_cols - 1)

    def down(k):
        return (me_col <= k) & (me_col > 0)

    def panel_out(k, i, src):
        @pl.when(up(k))
        def _():
            panel_hop(k, i, src, 1).start()

        if k:
            @pl.when(down(k))
            def _():
                panel_hop(k, i, src, -1).start()

    def panel_begin():
        for k in range(PANELS):
            @pl.when(me_col == k)
            def _(k=k):
                for i in chunks:
                    panel_out(k, i, panel_src(i))
                    pltpu.make_async_copy(panel_src(i), panel.at[k, i], panel_recv.at[k, i]).start()

    def panel_next(k, i, distance):
        @pl.when(jnp.abs(me_col - k) == distance)
        def _():
            wait(panel.at[k, i], panel_recv.at[k, i])
            if distance:
                panel_out(k, i, panel.at[k, i])

    def some_rows(which):
        return pl.ds(pl.multiple_of(which * (width // pair), width // pair), width // pair)

    def across_copy(k, slot, n):
        return remote(
            window.at[0, 0, some_rows(odd), slot, 0, :], across.at[k, slot, some_rows(odd)], across_send.at[k, slot],
            across_recv.at[k, slot], at(0, n, 0),
        )

    def across_begin():
        for k in range(PANELS):
            @pl.when(me_row == k)
            def _(k=k):
                for slot in range(col_blocks):
                    for n in range(1, grid_rows):
                        across_copy(k, slot, n).start()
                    pltpu.make_async_copy(window.at[0, 0, :, slot, 0, :], across.at[k, slot], across_recv.at[k, slot]).start()

    def across_half(k, slot):
        return across.at[k, slot, some_rows(odd)]

    def across_near(slot):
        for k in range(PANELS):
            @pl.when(me_row != k)
            def _(k=k):
                wait(across_half(k, slot), across_recv.at[k, slot])
                if pair > 1:
                    remote(across_half(k, slot), across_half(k, slot), half_send.at[k, slot], half_recv.at[k, slot], twin).start()

    def across_arrived(k, slot):
        @pl.when(me_row == k)
        def _():
            wait(across.at[k, slot], across_recv.at[k, slot])

        if pair > 1:
            @pl.when(me_row != k)
            def _():
                wait(across_half(k, slot), half_recv.at[k, slot])

    steps = half // STEP
    plan = [[] for _ in range(4 * steps)]
    plan[1].append(functools.partial(diag_pass, 1))
    plan[2].append(functools.partial(diag_pass, 2))
    plan[3].append(functools.partial(diag_pass, 3))
    plan[3].append(panel_begin)
    plan[4].append(across_begin)
    plan[5].append(functools.partial(diag_near, 2))
    plan[7].append(functools.partial(diag_near, 3))
    for slot in range(col_blocks):
        plan[min(12 + 2 * slot, 4 * steps - 1)].append(functools.partial(across_near, slot))
    final = []
    for distance in range(grid_cols):
        for i in chunks:
            for k in range(PANELS):
                when = 4 + 4 * distance + 2 * (i - skip) if distance else 4 * steps
                (plan[when] if when < 4 * steps else final).append(functools.partial(panel_next, k, i, distance))

    def hook(b):
        def run(s):
            for t in range(steps):
                if plan[b * steps + t]:
                    @pl.when(s == t)
                    def _(t=t):
                        for action in plan[b * steps + t]:
                            action()
        return run

    for p in range(len(PIECES)):
        diag_out(p)
    for copy in share_copies:
        copy.start()
    diag_pass(0)
    diag_arrived(0)

    def inverted(b, value):
        aug[...] = value
        invert(aug, half, hook(b))
        return aug[...]

    def joined(k, first, second, below):
        inverse[k, :half, :half] = first
        inverse[k, :half, half:] = jnp.zeros((half, half), jnp.float32)
        inverse[k, half:, half:] = second
        inverse[k, half:, :half] = -matmul(second, matmul(below, first))

    inv0 = inverted(0, diag[0, :half, :half])
    inverse[0, :half, :half] = inv0
    diag_arrived(1)
    below0 = matmul_t(diag[0, half:, :half], inv0)
    cross[:half, :half] = below0
    inv1 = inverted(1, diag[0, half:, half:] - matmul_t(below0, below0))
    diag_arrived(2)
    below0, inv0 = cross[:half, :half], inverse[0, :half, :half]
    cross0 = matmul_t(diag[1, :, :half], inv0)
    cross1 = matmul_t(diag[1, :, half:] - matmul_t(cross0, below0), inv1)
    cross[:, :half] = cross0
    cross[:, half:] = cross1
    joined(0, inv0, inv1, below0)
    diag_arrived(3)
    rest[...] = diag[2] - matmul_t(cross0, cross0) - matmul_t(cross1, cross1)
    inv2 = inverted(2, rest[:half, :half])
    inverse[1, :half, :half] = inv2
    below1 = matmul_t(rest[half:, :half], inv2)
    left[0, :half, :half] = below1
    inv3 = inverted(3, rest[half:, half:] - matmul_t(below1, below1))
    joined(1, inverse[1, :half, :half], inv3, left[0, :half, :half])

    for action in final:
        action()
    kept = (row_blocks - skip) * rows_here
    left[0, : kept] = matmul_t(panel[0, skip:].reshape(kept, width), inverse[0])
    left[1, : kept] = matmul_t(panel[1, skip:].reshape(kept, width) - update(left[0, :kept], cross[...], 1), inverse[1])
    row = lax.broadcasted_iota(jnp.int32, (rows_here, width), 0) + me_layer * rows_here
    lower = row >= lax.broadcasted_iota(jnp.int32, (rows_here, width), 1)
    factor0 = jnp.where(lower, matmul_t(diag[0, here, :], inverse[0]), 0.0)
    factor1 = jnp.where(lower, matmul_t(rest[here, :], inverse[1]), 0.0)
    plain0 = cross[here, :] if skip else left[0, :rows_here]
    plain1 = factor1 if skip else left[1, :rows_here]
    first0 = jnp.where(me_row == 0, factor0, plain0)
    first1 = jnp.where(me_row == 0, 0.0, jnp.where(me_row == 1, factor1, plain1))

    def out_copy(slot):
        return pltpu.make_async_copy(staged.at[slot], out.at[:, 0, :, slot, 0, :], out_sem.at[slot])

    for slot in range(col_blocks):
        for k in range(PANELS):
            across_arrived(k, slot)
        share_copies[slot].wait()
        right0 = matmul(inverse[0], across[0, slot])
        right1 = matmul(inverse[1], across[1, slot] - update(cross[...], right0, 0))
        number = slot * grid_cols + me_col
        updated = share[slot, skip:].reshape(kept, width)
        updated -= update(left[0, :kept], right0, 0) + update(left[1, :kept], right1, 0)
        value = jnp.where(number == 0, left[0, :kept], jnp.where(number == 1, left[1, :kept], updated))
        staged[slot, skip:] = value.reshape(row_blocks - skip, rows_here, width)
        plain = 0.0 if skip else jnp.where(me_row < PANELS, 0.0, updated[:rows_here])
        staged[slot, 0] = jnp.where(number == 0, first0, jnp.where(number == 1, first1, plain))
        out_copy(slot).start()

    for p in range(len(PIECES)):
        @pl.when(owners[p])
        def _(p=p):
            for col in range(grid_cols):
                wait(some(p, grid_rows if col else grid_rows - 1), diag_send.at[p, col])

        wait(some(p, len(targets(p))), pass_send.at[p])
        if shared(p):
            wait(some(p, layers * split // pair), near_send.at[p])
    for k in range(PANELS):
        @pl.when(up(k))
        def _(k=k):
            wait(panel.at[k, skip:], panel_send.at[k, 1])

        if k:
            @pl.when(down(k))
            def _(k=k):
                wait(panel.at[k, skip:], panel_send.at[k, 0])

        @pl.when(me_row == k)
        def _(k=k):
            for slot in range(col_blocks):
                for n in range(1, grid_rows):
                    wait(across_half(k, slot), across_send.at[k, slot])
    if pair > 1:
        for k in range(PANELS):
            @pl.when(me_row != k)
            def _(k=k):
                for slot in range(col_blocks):
                    wait(across_half(k, slot), half_send.at[k, slot])
    for slot in range(col_blocks):
        out_copy(slot).wait()


def local(sizes, schur_window):
    layers, grid_rows, grid_cols, row_blocks, col_blocks, width = sizes
    rows_here = width // layers
    anywhere = pl.BlockSpec(memory_space=pl.ANY)
    dma = pltpu.SemaphoreType.DMA
    pieces, diagonals, half = len(PIECES), len({p[2] for p in PIECES}), width // 2
    f32 = jnp.float32
    return pl.pallas_call(
        functools.partial(kernel, sizes),
        out_shape=jax.ShapeDtypeStruct((row_blocks, 1, rows_here, col_blocks, 1, width), f32),
        in_specs=[anywhere],
        out_specs=anywhere,
        scratch_shapes=[
            pltpu.VMEM((diagonals, width, width), f32),
            pltpu.VMEM((PANELS, col_blocks, width, width), f32),
            pltpu.VMEM((PANELS, row_blocks, rows_here, width), f32),
            pltpu.VMEM((col_blocks, row_blocks, rows_here, width), f32),
            pltpu.VMEM((col_blocks, row_blocks, rows_here, width), f32),
            pltpu.VMEM((half, half), f32),
            pltpu.VMEM((PANELS, width, width), f32),
            pltpu.VMEM((width, width), f32),
            pltpu.VMEM((width, width), f32),
            pltpu.VMEM((PANELS, row_blocks * rows_here, width), f32),
            dma((pieces, grid_cols)),
            dma((pieces,)),
            dma((pieces,)),
            dma((pieces,)),
            dma((pieces,)),
            dma((pieces,)),
            dma((PANELS, col_blocks)),
            dma((PANELS, col_blocks)),
            dma((PANELS, col_blocks)),
            dma((PANELS, col_blocks)),
            dma((PANELS, 2)),
            dma((PANELS, row_blocks)),
            dma((col_blocks,)),
            dma((col_blocks,)),
        ],
        compiler_params=pltpu.CompilerParams(collective_id=0, has_side_effects=True),
        name="window",
    )(schur_window)


def solution(mesh):
    def body(schur_window):
        row_blocks, _, width, col_blocks, _, _ = schur_window.shape
        sizes = (mesh.shape["layer"], mesh.shape["row"], mesh.shape["col"], row_blocks, col_blocks, width)
        return local(sizes, schur_window)

    return jax.shard_map(
        body,
        mesh=mesh,
        in_specs=(P(None, "row", None, None, "col", None),),
        out_specs=P(None, "row", "layer", None, "col", None),
        check_vma=False,
    )
```

```python
import functools

import jax
import jax.numpy as jnp
from jax import lax
from jax.experimental import pallas as pl
from jax.experimental.pallas import tpu as pltpu
from jax.sharding import PartitionSpec as P

PANELS = 2
SUB = 8
STEP = 32
SPAN = 2
SHARED = (2, 3)
PIECES = ((0, 0, 0, 0, 0), (0, 0, 0, 1, None), (1, 0, 1, None, None), (1, 1, 2, None, None))


def dot(a, b, lhs, rhs):
    return lax.dot_general(
        a, b, (((lhs,), (rhs,)), ((), ())),
        precision=lax.Precision.HIGHEST, preferred_element_type=jnp.float32,
    )


def matmul(a, b):
    return dot(a, b, 1, 0)


def matmul_t(a, b):
    return dot(a, b, 1, 1)


def update(a, b, rhs):
    a0, b0 = a.astype(jnp.bfloat16), b.astype(jnp.bfloat16)
    a1 = (a - a0.astype(jnp.float32)).astype(jnp.bfloat16)
    b1 = (b - b0.astype(jnp.float32)).astype(jnp.bfloat16)

    def product(x, y):
        return lax.dot_general(x, y, (((1,), (rhs,)), ((), ())), preferred_element_type=jnp.float32)

    return product(a0, b0) + (product(a0, b1) + product(a1, b0))


def spread(tile, start, count):
    size, lanes = tile.shape
    return [
        jnp.broadcast_to(tile[m // SUB * SUB :, start + m : start + m + 1], (size - m // SUB * SUB, lanes))
        for m in range(count)
    ]


def invert(aug, width, hook):
    sub = lax.broadcasted_iota(jnp.int32, (SUB, width), 0)
    lane = lax.broadcasted_iota(jnp.int32, (STEP, width), 1)
    row_in = lax.broadcasted_iota(jnp.int32, (STEP, width), 0)
    lane_below = lax.broadcasted_iota(jnp.int32, (width - STEP, width), 1)
    eye = jnp.where(lane == row_in, 1.0, 0.0).astype(jnp.float32)
    groups = STEP // SUB

    def step(s, carry):
        if hook is not None:
            hook(s)
        rest = aug[:STEP, :]
        below_rows = pltpu.roll(jnp.where(lane_below < STEP, 0.0, aug[STEP:, :]), width - STEP, 1)
        keep = row_in < STEP + s
        finished = []
        for g in range(groups):
            if g % SPAN == 0:
                column = spread(rest, g * SUB, SPAN * SUB)
                own = (lane >= g * SUB) & (lane < (g + SPAN) * SUB)
                rest = jnp.where(own[g * SUB :], eye[g * SUB :], rest)
                column = [jnp.where(keep[: c.shape[0]], c, 0.0) for c in column]
            rows = [jnp.broadcast_to(rest[j : j + 1, :], (SUB, width)) for j in range(SUB)]
            entry = [
                [jnp.broadcast_to(column[k][j : j + 1, :], (SUB, width)) if k >= j else None for k in range(SUB)]
                for j in range(SUB)
            ]
            done = jnp.zeros((SUB, width), jnp.float32)
            scales, lows = [], []
            for j in range(SUB):
                scale = lax.rsqrt(entry[j][j])
                rows[j] = rows[j] * scale
                done = jnp.where(sub == j, rows[j], done)
                low = [entry[j][k] * scale if k > j else None for k in range(SUB)]
                for k in range(j + 1, SUB):
                    for m in range(k, SUB):
                        entry[k][m] = entry[k][m] - low[k] * low[m]
                    rows[k] = rows[k] - low[k] * rows[j]
                scales.append(scale)
                lows.append(low)
            finished.append(done)
            after = groups - 1 - g
            if not after:
                break

            def tall(value):
                return jnp.concatenate([value] * after, axis=0) if after > 1 else value

            lower = []
            for j in range(SUB):
                c = column[j][SUB:, :]
                for i in range(j):
                    c = c - lower[i] * tall(lows[i][j])
                lower.append(c * tall(scales[j]))
            later = []
            for m in range(SUB, len(column)) if g % SPAN < SPAN - 1 else ():
                c = column[m]
                for j in range(SUB):
                    c = c - lower[j][m // SUB * SUB - SUB :, :] * lower[j][m - SUB : m - SUB + 1, :]
                later.append(c)
            rest = rest[SUB:, :]
            for j in range(SUB):
                rest = rest - lower[j] * tall(rows[j])
            column = later
        done = jnp.concatenate(finished, axis=0)
        done = jnp.where((lane < STEP) & (lane >= (row_in // (SPAN * SUB) + 1) * (SPAN * SUB)), 0.0, done)
        across = jnp.where((lane >= STEP) & (lane < width - s * STEP), done, 0.0)
        turned = pltpu.roll(done, width - STEP, 1)
        aug[: width - STEP, :] = below_rows - matmul(across.T[STEP:], turned)
        aug[width - STEP :, :] = turned
        return carry

    lax.fori_loop(0, width // STEP, step, 0)


def kernel(
    sizes, window, out, diag, across, panel, share, staged, aug, inverse, cross, rest, left,
    diag_send, diag_recv, pass_send, pass_recv, near_send, near_recv, across_send, across_recv, half_send, half_recv, panel_send,
    panel_recv, share_sem, out_sem,
):
    layers, grid_rows, grid_cols, row_blocks, col_blocks, width = sizes
    rows_here = width // layers
    half = width // 2
    split = 2 if grid_rows % 2 == 0 else 1
    skip = 1 if grid_rows <= PANELS else 0
    me_layer, me_row, me_col = lax.axis_index("layer"), lax.axis_index("row"), lax.axis_index("col")
    mine = lax.rem(me_row, split)
    pair = 2 if layers % 2 == 0 else 1
    odd = lax.rem(me_layer, pair)
    twin = (me_layer + 1 - 2 * odd, me_row, me_col)

    def at(layer, row, col):
        return (lax.rem(me_layer + layer, layers), lax.rem(me_row + row, grid_rows), lax.rem(me_col + col, grid_cols))

    def mate(layer, part):
        return (lax.rem(me_layer + layer, layers), me_row - mine + lax.rem(mine + part, split), me_col)

    def remote(src, dst, send, recv, target):
        return pltpu.make_async_remote_copy(
            src_ref=src, dst_ref=dst, send_sem=send, recv_sem=recv, device_id=target,
            device_id_type=pl.DeviceIdType.MESH,
        )

    def wait(ref, sem):
        pltpu.make_async_copy(ref, ref, sem).wait()

    here = pl.ds(pl.multiple_of(me_layer * rows_here, rows_here), rows_here)
    share_copies = [
        pltpu.make_async_copy(window.at[:, 0, here, slot, 0, :], share.at[slot], share_sem.at[slot])
        for slot in range(col_blocks)
    ]

    peers = [(row, col) for col in reversed(range(grid_cols)) for row in range(grid_rows) if row or col]
    mates = [(layer, part) for layer in range(layers) for part in range(split) if layer or part]
    barrier = pltpu.get_barrier_semaphore()
    for row, col in peers:
        pl.semaphore_signal(barrier, inc=1, device_id=at(0, row, col), device_id_type=pl.DeviceIdType.MESH)
    for layer, part in mates:
        if layer:
            pl.semaphore_signal(barrier, inc=1, device_id=mate(layer, part), device_id_type=pl.DeviceIdType.MESH)
    diag[0, :half, half:] = jnp.zeros((half, width - half), jnp.float32)
    pl.semaphore_wait(barrier, len(peers) + len(mates) - split + 1)

    def extent(p):
        _, _, slot, lower, side = PIECES[p]
        first, count = (0, width) if lower is None else (lower * half, half)
        return slot, first, count, pl.ds(0, width if side is None else half)

    def part_rows(p, part):
        _, first, count, _ = extent(p)
        size = count // (layers * split)
        return pl.ds(pl.multiple_of(first + (me_layer * split + part) * size, size), size)

    def diag_src(p, part):
        return window.at[0, 0, part_rows(p, part), 0, 0, extent(p)[3]]

    def diag_dst(p, part):
        return diag.at[extent(p)[0], part_rows(p, part), extent(p)[3]]

    def some(p, parts):
        slot, first, count, columns = extent(p)
        return diag.at[slot, pl.ds(first, parts * (count // (layers * split))), columns]

    def diag_copy(p, row, col):
        part = lax.rem(lax.rem(me_row + row, grid_rows), split)
        return remote(diag_src(p, part), diag_dst(p, part), diag_send.at[p, col], diag_recv.at[p], at(0, row, col))

    def diag_local(p):
        return pltpu.make_async_copy(diag_src(p, mine), diag_dst(p, mine), diag_recv.at[p])

    owners = [(me_row == piece[0]) & (me_col == piece[1]) for piece in PIECES]

    def diag_out(p):
        @pl.when(owners[p])
        def _():
            for row, col in peers:
                diag_copy(p, row, col).start()
            diag_local(p).start()

    def targets(p):
        return [m for m in mates if p not in SHARED or pair == 1 or m[0] % pair == 0]

    def stripe_rows(p, layer):
        _, first, count, _ = extent(p)
        size = count // layers
        return pl.ds(pl.multiple_of(first + lax.rem(me_layer + layer, layers) * size, size), size)

    def shared(p):
        return p in SHARED and pair > 1

    def diag_pass(p):
        wait(diag_dst(p, mine), diag_recv.at[p])
        for layer, part in targets(p):
            remote(diag_dst(p, mine), diag_dst(p, mine), pass_send.at[p], pass_recv.at[p], mate(layer, part)).start()

    def diag_near(p):
        if shared(p):
            wait(some(p, len(targets(p))), pass_recv.at[p])
            for layer in range(0, layers, pair):
                part = diag.at[extent(p)[0], stripe_rows(p, layer), extent(p)[3]]
                remote(part, part, near_send.at[p], near_recv.at[p], twin).start()

    def diag_arrived(p):
        if shared(p):
            wait(some(p, layers * split // pair), near_recv.at[p])
        else:
            wait(some(p, len(mates)), pass_recv.at[p])

    def panel_src(i):
        return window.at[i, 0, here, 0, 0, :]

    def panel_hop(k, i, src, way):
        return remote(src, panel.at[k, i], panel_send.at[k, 0 if way < 0 else 1], panel_recv.at[k, i], (me_layer, me_row, me_col + way))

    chunks = range(skip, row_blocks)

    def up(k):
        return (me_col >= k) & (me_col < grid_cols - 1)

    def down(k):
        return (me_col <= k) & (me_col > 0)

    def panel_out(k, i, src):
        @pl.when(up(k))
        def _():
            panel_hop(k, i, src, 1).start()

        if k:
            @pl.when(down(k))
            def _():
                panel_hop(k, i, src, -1).start()

    def panel_begin():
        for k in range(PANELS):
            @pl.when(me_col == k)
            def _(k=k):
                for i in chunks:
                    panel_out(k, i, panel_src(i))
                    pltpu.make_async_copy(panel_src(i), panel.at[k, i], panel_recv.at[k, i]).start()

    def panel_next(k, i, distance):
        @pl.when(jnp.abs(me_col - k) == distance)
        def _():
            wait(panel.at[k, i], panel_recv.at[k, i])
            if distance:
                panel_out(k, i, panel.at[k, i])

    def some_rows(which):
        return pl.ds(pl.multiple_of(which * (width // pair), width // pair), width // pair)

    def across_copy(k, slot, n):
        return remote(
            window.at[0, 0, some_rows(odd), slot, 0, :], across.at[k, slot, some_rows(odd)], across_send.at[k, slot],
            across_recv.at[k, slot], at(0, n, 0),
        )

    def across_begin():
        for k in range(PANELS):
            @pl.when(me_row == k)
            def _(k=k):
                for slot in range(col_blocks):
                    for n in range(1, grid_rows):
                        across_copy(k, slot, n).start()
                    pltpu.make_async_copy(window.at[0, 0, :, slot, 0, :], across.at[k, slot], across_recv.at[k, slot]).start()

    def across_half(k, slot):
        return across.at[k, slot, some_rows(odd)]

    def across_near(slot):
        for k in range(PANELS):
            @pl.when(me_row != k)
            def _(k=k):
                wait(across_half(k, slot), across_recv.at[k, slot])
                if pair > 1:
                    remote(across_half(k, slot), across_half(k, slot), half_send.at[k, slot], half_recv.at[k, slot], twin).start()

    def across_arrived(k, slot):
        @pl.when(me_row == k)
        def _():
            wait(across.at[k, slot], across_recv.at[k, slot])

        if pair > 1:
            @pl.when(me_row != k)
            def _():
                wait(across_half(k, slot), half_recv.at[k, slot])

    steps = half // STEP
    plan = [[] for _ in range(4 * steps)]
    plan[0].append(functools.partial(diag_pass, 1))
    plan[1].append(functools.partial(diag_pass, 2))
    plan[2].append(functools.partial(diag_pass, 3))
    plan[3].append(panel_begin)
    plan[4].append(functools.partial(diag_near, 2))
    plan[4].append(across_begin)
    plan[6].append(functools.partial(diag_near, 3))
    plan[12].append(functools.partial(across_near, 0))
    plan[14].append(functools.partial(across_near, 1))
    final = []
    for distance in range(grid_cols):
        for i in chunks:
            for k in range(PANELS):
                when = 6 + 3 * distance + (i - skip) if distance else 4 * steps
                (plan[when] if when < 4 * steps else final).append(functools.partial(panel_next, k, i, distance))

    def hook(b):
        def run(s):
            for t in range(steps):
                if plan[b * steps + t]:
                    @pl.when(s == t)
                    def _(t=t):
                        for action in plan[b * steps + t]:
                            action()
        return run

    for p in range(len(PIECES)):
        diag_out(p)
    for copy in share_copies:
        copy.start()
    diag_pass(0)
    diag_arrived(0)

    def inverted(b, value):
        aug[...] = value
        invert(aug, half, hook(b))
        return aug[...]

    def joined(k, first, second, below):
        inverse[k, :half, :half] = first
        inverse[k, :half, half:] = jnp.zeros((half, half), jnp.float32)
        inverse[k, half:, half:] = second
        inverse[k, half:, :half] = -matmul(second, matmul(below, first))

    inv0 = inverted(0, diag[0, :half, :half])
    inverse[0, :half, :half] = inv0
    diag_arrived(1)
    below0 = matmul_t(diag[0, half:, :half], inv0)
    cross[:half, :half] = below0
    inv1 = inverted(1, diag[0, half:, half:] - matmul_t(below0, below0))
    diag_arrived(2)
    below0, inv0 = cross[:half, :half], inverse[0, :half, :half]
    cross0 = matmul_t(diag[1, :, :half], inv0)
    cross1 = matmul_t(diag[1, :, half:] - matmul_t(cross0, below0), inv1)
    cross[:, :half] = cross0
    cross[:, half:] = cross1
    joined(0, inv0, inv1, below0)
    diag_arrived(3)
    rest[...] = diag[2] - matmul_t(cross0, cross0) - matmul_t(cross1, cross1)
    inv2 = inverted(2, rest[:half, :half])
    inverse[1, :half, :half] = inv2
    below1 = matmul_t(rest[half:, :half], inv2)
    left[0, :half, :half] = below1
    inv3 = inverted(3, rest[half:, half:] - matmul_t(below1, below1))
    joined(1, inverse[1, :half, :half], inv3, left[0, :half, :half])

    for action in final:
        action()
    kept = (row_blocks - skip) * rows_here
    left[0, : kept] = update(panel[0, skip:].reshape(kept, width), inverse[0], 1)
    left[1, : kept] = update(panel[1, skip:].reshape(kept, width) - update(left[0, :kept], cross[...], 1), inverse[1], 1)
    row = lax.broadcasted_iota(jnp.int32, (rows_here, width), 0) + me_layer * rows_here
    lower = row >= lax.broadcasted_iota(jnp.int32, (rows_here, width), 1)
    factor0 = jnp.where(lower, matmul_t(diag[0, here, :], inverse[0]), 0.0)
    factor1 = jnp.where(lower, matmul_t(rest[here, :], inverse[1]), 0.0)
    plain0 = cross[here, :] if skip else left[0, :rows_here]
    plain1 = factor1 if skip else left[1, :rows_here]
    first0 = jnp.where(me_row == 0, factor0, plain0)
    first1 = jnp.where(me_row == 0, 0.0, jnp.where(me_row == 1, factor1, plain1))

    def out_copy(slot):
        return pltpu.make_async_copy(staged.at[slot], out.at[:, 0, :, slot, 0, :], out_sem.at[slot])

    for slot in range(col_blocks):
        for k in range(PANELS):
            across_arrived(k, slot)
        share_copies[slot].wait()
        right0 = update(inverse[0], across[0, slot], 0)
        right1 = update(inverse[1], across[1, slot] - update(cross[...], right0, 0), 0)
        number = slot * grid_cols + me_col
        updated = share[slot, skip:].reshape(kept, width)
        updated -= update(left[0, :kept], right0, 0) + update(left[1, :kept], right1, 0)
        value = jnp.where(number == 0, left[0, :kept], jnp.where(number == 1, left[1, :kept], updated))
        staged[slot, skip:] = value.reshape(row_blocks - skip, rows_here, width)
        plain = 0.0 if skip else jnp.where(me_row < PANELS, 0.0, updated[:rows_here])
        staged[slot, 0] = jnp.where(number == 0, first0, jnp.where(number == 1, first1, plain))
        out_copy(slot).start()

    for p in range(len(PIECES)):
        @pl.when(owners[p])
        def _(p=p):
            for col in range(grid_cols):
                wait(some(p, grid_rows if col else grid_rows - 1), diag_send.at[p, col])

        wait(some(p, len(targets(p))), pass_send.at[p])
        if shared(p):
            wait(some(p, layers * split // pair), near_send.at[p])
    for k in range(PANELS):
        @pl.when(up(k))
        def _(k=k):
            wait(panel.at[k, skip:], panel_send.at[k, 1])

        if k:
            @pl.when(down(k))
            def _(k=k):
                wait(panel.at[k, skip:], panel_send.at[k, 0])

        @pl.when(me_row == k)
        def _(k=k):
            for slot in range(col_blocks):
                for n in range(1, grid_rows):
                    wait(across_half(k, slot), across_send.at[k, slot])
    if pair > 1:
        for k in range(PANELS):
            @pl.when(me_row != k)
            def _(k=k):
                for slot in range(col_blocks):
                    wait(across_half(k, slot), half_send.at[k, slot])
    for slot in range(col_blocks):
        out_copy(slot).wait()


def local(sizes, schur_window):
    layers, grid_rows, grid_cols, row_blocks, col_blocks, width = sizes
    rows_here = width // layers
    anywhere = pl.BlockSpec(memory_space=pl.ANY)
    dma = pltpu.SemaphoreType.DMA
    pieces, diagonals, half = len(PIECES), len({p[2] for p in PIECES}), width // 2
    f32 = jnp.float32
    return pl.pallas_call(
        functools.partial(kernel, sizes),
        out_shape=jax.ShapeDtypeStruct((row_blocks, 1, rows_here, col_blocks, 1, width), f32),
        in_specs=[anywhere],
        out_specs=anywhere,
        scratch_shapes=[
            pltpu.VMEM((diagonals, width, width), f32),
            pltpu.VMEM((PANELS, col_blocks, width, width), f32),
            pltpu.VMEM((PANELS, row_blocks, rows_here, width), f32),
            pltpu.VMEM((col_blocks, row_blocks, rows_here, width), f32),
            pltpu.VMEM((col_blocks, row_blocks, rows_here, width), f32),
            pltpu.VMEM((half, half), f32),
            pltpu.VMEM((PANELS, width, width), f32),
            pltpu.VMEM((width, width), f32),
            pltpu.VMEM((width, width), f32),
            pltpu.VMEM((PANELS, row_blocks * rows_here, width), f32),
            dma((pieces, grid_cols)),
            dma((pieces,)),
            dma((pieces,)),
            dma((pieces,)),
            dma((pieces,)),
            dma((pieces,)),
            dma((PANELS, col_blocks)),
            dma((PANELS, col_blocks)),
            dma((PANELS, col_blocks)),
            dma((PANELS, col_blocks)),
            dma((PANELS, 2)),
            dma((PANELS, row_blocks)),
            dma((col_blocks,)),
            dma((col_blocks,)),
        ],
        compiler_params=pltpu.CompilerParams(collective_id=0, has_side_effects=True),
        name="window",
    )(schur_window)


def solution(mesh):
    def body(schur_window):
        row_blocks, _, width, col_blocks, _, _ = schur_window.shape
        sizes = (mesh.shape["layer"], mesh.shape["row"], mesh.shape["col"], row_blocks, col_blocks, width)
        return local(sizes, schur_window)

    return jax.shard_map(
        body,
        mesh=mesh,
        in_specs=(P(None, "row", None, None, "col", None),),
        out_specs=P(None, "row", "layer", None, "col", None),
        check_vma=False,
    )
```

```python
import functools

import jax
import jax.numpy as jnp
from jax import lax
from jax.experimental import pallas as pl
from jax.experimental.pallas import tpu as pltpu
from jax.sharding import PartitionSpec as P

PANELS = 2
SUB = 8
STEP = 32
SPAN = 2
SHARED = (2, 3)
ORDER = (0, 1, 2, 3)
PANEL = 1
ACROSS = 4
HOP = 6
HOPS = 3
PIECES = ((0, 0, 0, 0, 0), (0, 0, 0, 1, None), (1, 0, 1, None, None), (1, 1, 2, None, None))


def dot(a, b, lhs, rhs):
    return lax.dot_general(
        a, b, (((lhs,), (rhs,)), ((), ())),
        precision=lax.Precision.HIGHEST, preferred_element_type=jnp.float32,
    )


def matmul(a, b):
    return dot(a, b, 1, 0)


def matmul_t(a, b):
    return dot(a, b, 1, 1)


def update(a, b, rhs):
    a0, b0 = a.astype(jnp.bfloat16), b.astype(jnp.bfloat16)
    a1 = (a - a0.astype(jnp.float32)).astype(jnp.bfloat16)
    b1 = (b - b0.astype(jnp.float32)).astype(jnp.bfloat16)

    def product(x, y):
        return lax.dot_general(x, y, (((1,), (rhs,)), ((), ())), preferred_element_type=jnp.float32)

    return product(a0, b0) + (product(a0, b1) + product(a1, b0))


def spread(tile, start, count):
    size, lanes = tile.shape
    return [
        jnp.broadcast_to(tile[m // SUB * SUB :, start + m : start + m + 1], (size - m // SUB * SUB, lanes))
        for m in range(count)
    ]


def invert(aug, width, hook):
    sub = lax.broadcasted_iota(jnp.int32, (SUB, width), 0)
    lane = lax.broadcasted_iota(jnp.int32, (STEP, width), 1)
    row_in = lax.broadcasted_iota(jnp.int32, (STEP, width), 0)
    lane_below = lax.broadcasted_iota(jnp.int32, (width - STEP, width), 1)
    eye = jnp.where(lane == row_in, 1.0, 0.0).astype(jnp.float32)
    groups = STEP // SUB

    def step(s, carry):
        if hook is not None:
            hook(s)
        rest = aug[:STEP, :]
        below_rows = pltpu.roll(jnp.where(lane_below < STEP, 0.0, aug[STEP:, :]), width - STEP, 1)
        keep = row_in < STEP + s
        finished = []
        for g in range(groups):
            if g % SPAN == 0:
                column = spread(rest, g * SUB, SPAN * SUB)
                own = (lane >= g * SUB) & (lane < (g + SPAN) * SUB)
                rest = jnp.where(own[g * SUB :], eye[g * SUB :], rest)
                column = [jnp.where(keep[: c.shape[0]], c, 0.0) for c in column]
            rows = [jnp.broadcast_to(rest[j : j + 1, :], (SUB, width)) for j in range(SUB)]
            entry = [
                [jnp.broadcast_to(column[k][j : j + 1, :], (SUB, width)) if k >= j else None for k in range(SUB)]
                for j in range(SUB)
            ]
            done = jnp.zeros((SUB, width), jnp.float32)
            scales, lows = [], []
            for j in range(SUB):
                scale = lax.rsqrt(entry[j][j])
                rows[j] = rows[j] * scale
                done = jnp.where(sub == j, rows[j], done)
                low = [entry[j][k] * scale if k > j else None for k in range(SUB)]
                for k in range(j + 1, SUB):
                    for m in range(k, SUB):
                        entry[k][m] = entry[k][m] - low[k] * low[m]
                    rows[k] = rows[k] - low[k] * rows[j]
                scales.append(scale)
                lows.append(low)
            finished.append(done)
            after = groups - 1 - g
            if not after:
                break

            def tall(value):
                return jnp.concatenate([value] * after, axis=0) if after > 1 else value

            lower = []
            for j in range(SUB):
                c = column[j][SUB:, :]
                for i in range(j):
                    c = c - lower[i] * tall(lows[i][j])
                lower.append(c * tall(scales[j]))
            later = []
            for m in range(SUB, len(column)) if g % SPAN < SPAN - 1 else ():
                c = column[m]
                for j in range(SUB):
                    c = c - lower[j][m // SUB * SUB - SUB :, :] * lower[j][m - SUB : m - SUB + 1, :]
                later.append(c)
            rest = rest[SUB:, :]
            for j in range(SUB):
                rest = rest - lower[j] * tall(rows[j])
            column = later
        done = jnp.concatenate(finished, axis=0)
        done = jnp.where((lane < STEP) & (lane >= (row_in // (SPAN * SUB) + 1) * (SPAN * SUB)), 0.0, done)
        across = jnp.where((lane >= STEP) & (lane < width - s * STEP), done, 0.0)
        turned = pltpu.roll(done, width - STEP, 1)
        aug[: width - STEP, :] = below_rows - matmul(across.T[STEP:], turned)
        aug[width - STEP :, :] = turned
        return carry

    lax.fori_loop(0, width // STEP, step, 0)


def kernel(
    sizes, window, out, diag, across, panel, share, staged, aug, inverse, cross, rest, left, peer_ready, mate_ready,
    diag_send, diag_recv, pass_send, pass_recv, near_send, near_recv, across_send, across_recv, half_send, half_recv, panel_send,
    panel_recv, share_sem, out_sem,
):
    layers, grid_rows, grid_cols, row_blocks, col_blocks, width = sizes
    rows_here = width // layers
    half = width // 2
    split = 2 if grid_rows % 2 == 0 else 1
    skip = 1 if grid_rows <= PANELS else 0
    me_layer, me_row, me_col = lax.axis_index("layer"), lax.axis_index("row"), lax.axis_index("col")
    mine = lax.rem(me_row, split)
    pair = 2 if layers % 2 == 0 else 1
    odd = lax.rem(me_layer, pair)
    twin = (me_layer + 1 - 2 * odd, me_row, me_col)

    def at(layer, row, col):
        return (lax.rem(me_layer + layer, layers), lax.rem(me_row + row, grid_rows), lax.rem(me_col + col, grid_cols))

    def mate(layer, part):
        return (lax.rem(me_layer + layer, layers), me_row - mine + lax.rem(mine + part, split), me_col)

    def remote(src, dst, send, recv, target):
        return pltpu.make_async_remote_copy(
            src_ref=src, dst_ref=dst, send_sem=send, recv_sem=recv, device_id=target,
            device_id_type=pl.DeviceIdType.MESH,
        )

    def wait(ref, sem):
        pltpu.make_async_copy(ref, ref, sem).wait()

    here = pl.ds(pl.multiple_of(me_layer * rows_here, rows_here), rows_here)
    share_copies = [
        pltpu.make_async_copy(window.at[:, 0, here, slot, 0, :], share.at[slot], share_sem.at[slot])
        for slot in range(col_blocks)
    ]

    peers = [(row, col) for col in reversed(range(grid_cols)) for row in range(grid_rows) if row or col]
    mates = [(layer, part) for layer in range(layers) for part in range(split) if layer or part]
    diag[0, :half, half:] = jnp.zeros((half, width - half), jnp.float32)
    def signal(sem, target):
        pl.semaphore_signal(sem, inc=1, device_id=target, device_id_type=pl.DeviceIdType.MESH)

    def peer_after(row, col):
        _, other_row, other_col = at(0, row, col)
        return (other_col > me_col) | ((other_col == me_col) & (other_row > me_row))

    def mate_after(layer):
        return lax.rem(me_layer + layer, layers) > me_layer

    def owner(row, col):
        found = (row == PIECES[1][0]) & (col == PIECES[1][1])
        for i, j, *_ in PIECES[2:]:
            found = found | ((row == i) & (col == j))
        return found

    def known(row, col):
        return col == 0 or (row == 0 and col == 1)

    def talks(row, col, sender_row, sender_col):
        if known(row, col):
            return True
        return owner(sender_row, sender_col)

    far_mates = [(layer, part) for layer, part in mates if layer]
    barrier = pltpu.get_barrier_semaphore()
    for row, col in peers:
        @pl.when(peer_after(row, col))
        def _(row=row, col=col):
            signal(barrier, at(0, row, col))
    for layer, part in far_mates:
        @pl.when(mate_after(layer))
        def _(layer=layer, part=part):
            signal(barrier, mate(layer, part))
    before = me_col * grid_rows + me_row + me_layer * split

    @pl.when(before > 0)
    def _():
        pl.semaphore_wait(barrier, before)

    for row, col in peers:
        back = (-row % grid_rows, -col % grid_cols)
        _, to_row, to_col = at(0, row, col)

        @pl.when(jnp.logical_not(peer_after(row, col)) & talks(*back, to_row, to_col))
        def _(row=row, col=col, back=back):
            signal(peer_ready.at[back[0], back[1]], at(0, row, col))
    for layer, part in far_mates:
        @pl.when(jnp.logical_not(mate_after(layer)))
        def _(layer=layer, part=part):
            signal(mate_ready.at[-layer % layers, -part % split], mate(layer, part))

    def peer_entered(row, col):
        @pl.when(peer_after(row, col) & talks(row, col, me_row, me_col))
        def _():
            pl.semaphore_wait(peer_ready.at[row, col], 1)

    def mates_entered():
        for layer, part in far_mates:
            @pl.when(mate_after(layer))
            def _(layer=layer, part=part):
                pl.semaphore_wait(mate_ready.at[layer, part], 1)

    def peers_entered(mine_too):
        for row, col in peers:
            if known(row, col) == (not mine_too):
                peer_entered(row, col)

    def extent(p):
        _, _, slot, lower, side = PIECES[p]
        first, count = (0, width) if lower is None else (lower * half, half)
        return slot, first, count, pl.ds(0, width if side is None else half)

    def part_rows(p, part):
        _, first, count, _ = extent(p)
        size = count // (layers * split)
        return pl.ds(pl.multiple_of(first + (me_layer * split + part) * size, size), size)

    def diag_src(p, part):
        return window.at[0, 0, part_rows(p, part), 0, 0, extent(p)[3]]

    def diag_dst(p, part):
        return diag.at[extent(p)[0], part_rows(p, part), extent(p)[3]]

    def some(p, parts):
        slot, first, count, columns = extent(p)
        return diag.at[slot, pl.ds(first, parts * (count // (layers * split))), columns]

    def diag_copy(p, row, col):
        part = lax.rem(lax.rem(me_row + row, grid_rows), split)
        return remote(diag_src(p, part), diag_dst(p, part), diag_send.at[p, col], diag_recv.at[p], at(0, row, col))

    def diag_local(p):
        return pltpu.make_async_copy(diag_src(p, mine), diag_dst(p, mine), diag_recv.at[p])

    owners = [(me_row == piece[0]) & (me_col == piece[1]) for piece in PIECES]

    def whole(p):
        return PIECES[p][:2] == PIECES[0][:2]

    def here_whole(p):
        return me_col == PIECES[p][1]

    def full(ref, p):
        slot, first, count, columns = extent(p)
        return ref.at[0, 0, pl.ds(first, count), 0, 0, columns] if ref is window else ref.at[slot, pl.ds(first, count), columns]

    def diag_out(p):
        @pl.when(owners[p])
        def _():
            for col in range(grid_cols):
                for row in range(grid_rows):
                    if not (row or col):
                        continue
                    if col == 0 and whole(p):
                        remote(full(window, p), full(diag, p), diag_send.at[p, col], diag_recv.at[p], at(0, row, col)).start()
                    else:
                        diag_copy(p, row, col).start()
            if whole(p):
                pltpu.make_async_copy(full(window, p), full(diag, p), diag_recv.at[p]).start()
            else:
                diag_local(p).start()

    def targets(p):
        return [m for m in mates if p not in SHARED or pair == 1 or m[0] % pair == 0]

    def stripe_rows(p, layer):
        _, first, count, _ = extent(p)
        size = count // layers
        return pl.ds(pl.multiple_of(first + lax.rem(me_layer + layer, layers) * size, size), size)

    def shared(p):
        return p in SHARED and pair > 1

    def diag_pass(p):
        def run():
            wait(diag_dst(p, mine), diag_recv.at[p])
            for layer, part in targets(p):
                remote(diag_dst(p, mine), diag_dst(p, mine), pass_send.at[p], pass_recv.at[p], mate(layer, part)).start()

        if whole(p):
            pl.when(jnp.logical_not(here_whole(p)))(run)
        else:
            run()

    def diag_near(p):
        if shared(p):
            wait(some(p, len(targets(p))), pass_recv.at[p])
            for layer in range(0, layers, pair):
                part = diag.at[extent(p)[0], stripe_rows(p, layer), extent(p)[3]]
                remote(part, part, near_send.at[p], near_recv.at[p], twin).start()

    def diag_arrived(p):
        if shared(p):
            wait(some(p, layers * split // pair), near_recv.at[p])
        elif whole(p):
            @pl.when(here_whole(p))
            def _():
                wait(full(diag, p), diag_recv.at[p])

            @pl.when(jnp.logical_not(here_whole(p)))
            def _():
                wait(some(p, len(mates)), pass_recv.at[p])
        else:
            wait(some(p, len(mates)), pass_recv.at[p])

    def panel_src(i):
        return window.at[i, 0, here, 0, 0, :]

    def panel_hop(k, i, src, way):
        return remote(src, panel.at[k, i], panel_send.at[k, 0 if way < 0 else 1], panel_recv.at[k, i], (me_layer, me_row, me_col + way))

    chunks = range(skip, row_blocks)

    def up(k):
        return (me_col >= k) & (me_col < grid_cols - 1)

    def down(k):
        return (me_col <= k) & (me_col > 0)

    def panel_out(k, i, src):
        @pl.when(up(k))
        def _():
            panel_hop(k, i, src, 1).start()

        if k:
            @pl.when(down(k))
            def _():
                panel_hop(k, i, src, -1).start()

    def panel_begin():
        for k in range(PANELS):
            @pl.when(me_col == k)
            def _(k=k):
                for i in chunks:
                    panel_out(k, i, panel_src(i))
                    pltpu.make_async_copy(panel_src(i), panel.at[k, i], panel_recv.at[k, i]).start()

    def passes(k):
        return ((me_col > k) & (me_col < grid_cols - 1)) | ((me_col < k) & (me_col > 0))

    def panel_next(k, i, distance):
        @pl.when(passes(k) & (jnp.abs(me_col - k) == distance))
        def _():
            wait(panel.at[k, i], panel_recv.at[k, i])
            panel_out(k, i, panel.at[k, i])

    def panel_arrived(k, i):
        @pl.when(jnp.logical_not(passes(k)))
        def _():
            wait(panel.at[k, i], panel_recv.at[k, i])

    def some_rows(which):
        return pl.ds(pl.multiple_of(which * (width // pair), width // pair), width // pair)

    def across_copy(k, slot, n):
        return remote(
            window.at[0, 0, some_rows(odd), slot, 0, :], across.at[k, slot, some_rows(odd)], across_send.at[k, slot],
            across_recv.at[k, slot], at(0, n, 0),
        )

    def across_begin():
        for k in range(PANELS):
            @pl.when(me_row == k)
            def _(k=k):
                for slot in range(col_blocks):
                    for n in range(1, grid_rows):
                        across_copy(k, slot, n).start()
                    pltpu.make_async_copy(window.at[0, 0, :, slot, 0, :], across.at[k, slot], across_recv.at[k, slot]).start()

    def across_half(k, slot):
        return across.at[k, slot, some_rows(odd)]

    def across_near(slot):
        for k in range(PANELS):
            @pl.when(me_row != k)
            def _(k=k):
                wait(across_half(k, slot), across_recv.at[k, slot])
                if pair > 1:
                    remote(across_half(k, slot), across_half(k, slot), half_send.at[k, slot], half_recv.at[k, slot], twin).start()

    def across_arrived(k, slot):
        @pl.when(me_row == k)
        def _():
            wait(across.at[k, slot], across_recv.at[k, slot])

        if pair > 1:
            @pl.when(me_row != k)
            def _():
                wait(across_half(k, slot), half_recv.at[k, slot])

    steps = half // STEP
    plan = [[] for _ in range(4 * steps)]
    def mates_first():
        pl.when(here_whole(0))(mates_entered)

    plan[0].append(functools.partial(diag_pass, 1))
    plan[0].append(mates_first)
    plan[1].append(functools.partial(diag_pass, 2))
    plan[2].append(functools.partial(diag_pass, 3))
    plan[PANEL].append(panel_begin)
    plan[4].append(functools.partial(diag_near, 2))
    plan[ACROSS].append(across_begin)
    plan[6].append(functools.partial(diag_near, 3))
    plan[12].append(functools.partial(across_near, 0))
    plan[14].append(functools.partial(across_near, 1))
    final = []
    for distance in range(1, grid_cols):
        for i in chunks:
            for k in range(PANELS):
                when = HOP + HOPS * (distance - 1) + (i - skip)
                (plan[when] if when < 4 * steps else final).append(functools.partial(panel_next, k, i, distance))
    for i in chunks:
        for k in range(PANELS):
            final.append(functools.partial(panel_arrived, k, i))

    def hook(b):
        def run(s):
            for t in range(steps):
                if plan[b * steps + t]:
                    @pl.when(s == t)
                    def _(t=t):
                        for action in plan[b * steps + t]:
                            action()
        return run

    @pl.when(owner(me_row, me_col))
    def _():
        peers_entered(True)

    peers_entered(False)
    for p in ORDER:
        diag_out(p)

    @pl.when(jnp.logical_not(here_whole(0)))
    def _():
        mates_entered()

    diag_pass(0)
    for copy in share_copies:
        copy.start()
    diag_arrived(0)

    def inverted(b, value):
        aug[...] = value
        invert(aug, half, hook(b))
        return aug[...]

    def joined(k, first, second, below):
        inverse[k, :half, :half] = first
        inverse[k, :half, half:] = jnp.zeros((half, half), jnp.float32)
        inverse[k, half:, half:] = second
        inverse[k, half:, :half] = -matmul(second, matmul(below, first))

    inv0 = inverted(0, diag[0, :half, :half])
    inverse[0, :half, :half] = inv0
    diag_arrived(1)
    below0 = matmul_t(diag[0, half:, :half], inv0)
    cross[:half, :half] = below0
    inv1 = inverted(1, diag[0, half:, half:] - matmul_t(below0, below0))
    diag_arrived(2)
    below0, inv0 = cross[:half, :half], inverse[0, :half, :half]
    cross0 = matmul_t(diag[1, :, :half], inv0)
    cross1 = matmul_t(diag[1, :, half:] - matmul_t(cross0, below0), inv1)
    cross[:, :half] = cross0
    cross[:, half:] = cross1
    joined(0, inv0, inv1, below0)
    diag_arrived(3)
    rest[...] = diag[2] - matmul_t(cross0, cross0) - matmul_t(cross1, cross1)
    inv2 = inverted(2, rest[:half, :half])
    inverse[1, :half, :half] = inv2
    below1 = matmul_t(rest[half:, :half], inv2)
    left[0, :half, :half] = below1
    inv3 = inverted(3, rest[half:, half:] - matmul_t(below1, below1))
    joined(1, inverse[1, :half, :half], inv3, left[0, :half, :half])

    for action in final:
        action()
    kept = (row_blocks - skip) * rows_here
    left[0, : kept] = update(panel[0, skip:].reshape(kept, width), inverse[0], 1)
    left[1, : kept] = update(panel[1, skip:].reshape(kept, width) - update(left[0, :kept], cross[...], 1), inverse[1], 1)
    row = lax.broadcasted_iota(jnp.int32, (rows_here, width), 0) + me_layer * rows_here
    lower = row >= lax.broadcasted_iota(jnp.int32, (rows_here, width), 1)
    factor0 = jnp.where(lower, matmul_t(diag[0, here, :], inverse[0]), 0.0)
    factor1 = jnp.where(lower, matmul_t(rest[here, :], inverse[1]), 0.0)
    plain0 = cross[here, :] if skip else left[0, :rows_here]
    plain1 = factor1 if skip else left[1, :rows_here]
    first0 = jnp.where(me_row == 0, factor0, plain0)
    first1 = jnp.where(me_row == 0, 0.0, jnp.where(me_row == 1, factor1, plain1))

    def out_copy(slot):
        return pltpu.make_async_copy(staged.at[slot], out.at[:, 0, :, slot, 0, :], out_sem.at[slot])

    for slot in range(col_blocks):
        for k in range(PANELS):
            across_arrived(k, slot)
        share_copies[slot].wait()
        right0 = update(inverse[0], across[0, slot], 0)
        right1 = update(inverse[1], across[1, slot] - update(cross[...], right0, 0), 0)
        number = slot * grid_cols + me_col
        updated = share[slot, skip:].reshape(kept, width)
        updated -= update(left[0, :kept], right0, 0) + update(left[1, :kept], right1, 0)
        value = jnp.where(number == 0, left[0, :kept], jnp.where(number == 1, left[1, :kept], updated))
        staged[slot, skip:] = value.reshape(row_blocks - skip, rows_here, width)
        plain = 0.0 if skip else jnp.where(me_row < PANELS, 0.0, updated[:rows_here])
        staged[slot, 0] = jnp.where(number == 0, first0, jnp.where(number == 1, first1, plain))
        out_copy(slot).start()

    for p in range(len(PIECES)):
        @pl.when(owners[p])
        def _(p=p):
            for col in range(grid_cols):
                if col == 0 and whole(p):
                    for _ in range(1, grid_rows):
                        wait(full(diag, p), diag_send.at[p, col])
                else:
                    wait(some(p, grid_rows if col else grid_rows - 1), diag_send.at[p, col])

        def sent(p=p):
            wait(some(p, len(targets(p))), pass_send.at[p])

        if whole(p):
            pl.when(jnp.logical_not(here_whole(p)))(sent)
        else:
            sent()
        if shared(p):
            wait(some(p, layers * split // pair), near_send.at[p])
    for k in range(PANELS):
        @pl.when(up(k))
        def _(k=k):
            wait(panel.at[k, skip:], panel_send.at[k, 1])

        if k:
            @pl.when(down(k))
            def _(k=k):
                wait(panel.at[k, skip:], panel_send.at[k, 0])

        @pl.when(me_row == k)
        def _(k=k):
            for slot in range(col_blocks):
                for n in range(1, grid_rows):
                    wait(across_half(k, slot), across_send.at[k, slot])
    if pair > 1:
        for k in range(PANELS):
            @pl.when(me_row != k)
            def _(k=k):
                for slot in range(col_blocks):
                    wait(across_half(k, slot), half_send.at[k, slot])
    for slot in range(col_blocks):
        out_copy(slot).wait()


def local(sizes, schur_window):
    layers, grid_rows, grid_cols, row_blocks, col_blocks, width = sizes
    rows_here = width // layers
    anywhere = pl.BlockSpec(memory_space=pl.ANY)
    dma = pltpu.SemaphoreType.DMA
    pieces, diagonals, half = len(PIECES), len({p[2] for p in PIECES}), width // 2
    split = 2 if grid_rows % 2 == 0 else 1
    f32 = jnp.float32
    return pl.pallas_call(
        functools.partial(kernel, sizes),
        out_shape=jax.ShapeDtypeStruct((row_blocks, 1, rows_here, col_blocks, 1, width), f32),
        in_specs=[anywhere],
        out_specs=anywhere,
        scratch_shapes=[
            pltpu.VMEM((diagonals, width, width), f32),
            pltpu.VMEM((PANELS, col_blocks, width, width), f32),
            pltpu.VMEM((PANELS, row_blocks, rows_here, width), f32),
            pltpu.VMEM((col_blocks, row_blocks, rows_here, width), f32),
            pltpu.VMEM((col_blocks, row_blocks, rows_here, width), f32),
            pltpu.VMEM((half, half), f32),
            pltpu.VMEM((PANELS, width, width), f32),
            pltpu.VMEM((width, width), f32),
            pltpu.VMEM((width, width), f32),
            pltpu.VMEM((PANELS, row_blocks * rows_here, width), f32),
            pltpu.SemaphoreType.REGULAR((grid_rows, grid_cols)),
            pltpu.SemaphoreType.REGULAR((layers, split)),
            dma((pieces, grid_cols)),
            dma((pieces,)),
            dma((pieces,)),
            dma((pieces,)),
            dma((pieces,)),
            dma((pieces,)),
            dma((PANELS, col_blocks)),
            dma((PANELS, col_blocks)),
            dma((PANELS, col_blocks)),
            dma((PANELS, col_blocks)),
            dma((PANELS, 2)),
            dma((PANELS, row_blocks)),
            dma((col_blocks,)),
            dma((col_blocks,)),
        ],
        compiler_params=pltpu.CompilerParams(collective_id=0, has_side_effects=True),
        name="window",
    )(schur_window)


def solution(mesh):
    def body(schur_window):
        row_blocks, _, width, col_blocks, _, _ = schur_window.shape
        sizes = (mesh.shape["layer"], mesh.shape["row"], mesh.shape["col"], row_blocks, col_blocks, width)
        return local(sizes, schur_window)

    return jax.shard_map(
        body,
        mesh=mesh,
        in_specs=(P(None, "row", None, None, "col", None),),
        out_specs=P(None, "row", "layer", None, "col", None),
        check_vma=False,
    )
```

```python
import functools

import jax
import jax.numpy as jnp
from jax import lax
from jax.experimental import pallas as pl
from jax.experimental.pallas import tpu as pltpu
from jax.sharding import PartitionSpec as P

PANELS = 2
SUB = 8
STEP = 32
SPAN = 2
SHARED = (2, 3)
ORDER = (0, 1, 2, 3)
PANEL = 1
ACROSS = 6
HOP = 6
HOPS = 3
PIECES = ((0, 0, 0, 0, 0), (0, 0, 0, 1, None), (1, 0, 1, None, None), (1, 1, 2, None, None))


def dot(a, b, lhs, rhs):
    return lax.dot_general(
        a, b, (((lhs,), (rhs,)), ((), ())),
        precision=lax.Precision.HIGHEST, preferred_element_type=jnp.float32,
    )


def matmul(a, b):
    return dot(a, b, 1, 0)


def matmul_t(a, b):
    return dot(a, b, 1, 1)


def update(a, b, rhs):
    a0, b0 = a.astype(jnp.bfloat16), b.astype(jnp.bfloat16)
    a1 = (a - a0.astype(jnp.float32)).astype(jnp.bfloat16)
    b1 = (b - b0.astype(jnp.float32)).astype(jnp.bfloat16)

    def product(x, y):
        return lax.dot_general(x, y, (((1,), (rhs,)), ((), ())), preferred_element_type=jnp.float32)

    return product(a0, b0) + (product(a0, b1) + product(a1, b0))


def spread(tile, start, count):
    size, lanes = tile.shape
    return [
        jnp.broadcast_to(tile[m // SUB * SUB :, start + m : start + m + 1], (size - m // SUB * SUB, lanes))
        for m in range(count)
    ]


def invert(aug, width, hook):
    sub = lax.broadcasted_iota(jnp.int32, (SUB, width), 0)
    lane = lax.broadcasted_iota(jnp.int32, (STEP, width), 1)
    row_in = lax.broadcasted_iota(jnp.int32, (STEP, width), 0)
    lane_below = lax.broadcasted_iota(jnp.int32, (width - STEP, width), 1)
    eye = jnp.where(lane == row_in, 1.0, 0.0).astype(jnp.float32)
    groups = STEP // SUB

    def step(s, carry):
        if hook is not None:
            hook(s)
        rest = aug[:STEP, :]
        below_rows = pltpu.roll(jnp.where(lane_below < STEP, 0.0, aug[STEP:, :]), width - STEP, 1)
        keep = row_in < STEP + s
        finished = []
        for g in range(groups):
            if g % SPAN == 0:
                column = spread(rest, g * SUB, SPAN * SUB)
                own = (lane >= g * SUB) & (lane < (g + SPAN) * SUB)
                rest = jnp.where(own[g * SUB :], eye[g * SUB :], rest)
                column = [jnp.where(keep[: c.shape[0]], c, 0.0) for c in column]
            rows = [jnp.broadcast_to(rest[j : j + 1, :], (SUB, width)) for j in range(SUB)]
            entry = [
                [jnp.broadcast_to(column[k][j : j + 1, :], (SUB, width)) if k >= j else None for k in range(SUB)]
                for j in range(SUB)
            ]
            done = jnp.zeros((SUB, width), jnp.float32)
            scales, lows = [], []
            for j in range(SUB):
                scale = lax.rsqrt(entry[j][j])
                rows[j] = rows[j] * scale
                done = jnp.where(sub == j, rows[j], done)
                low = [entry[j][k] * scale if k > j else None for k in range(SUB)]
                for k in range(j + 1, SUB):
                    for m in range(k, SUB):
                        entry[k][m] = entry[k][m] - low[k] * low[m]
                    rows[k] = rows[k] - low[k] * rows[j]
                scales.append(scale)
                lows.append(low)
            finished.append(done)
            after = groups - 1 - g
            if not after:
                break

            def tall(value):
                return jnp.concatenate([value] * after, axis=0) if after > 1 else value

            lower = []
            for j in range(SUB):
                c = column[j][SUB:, :]
                for i in range(j):
                    c = c - lower[i] * tall(lows[i][j])
                lower.append(c * tall(scales[j]))
            later = []
            for m in range(SUB, len(column)) if g % SPAN < SPAN - 1 else ():
                c = column[m]
                for j in range(SUB):
                    c = c - lower[j][m // SUB * SUB - SUB :, :] * lower[j][m - SUB : m - SUB + 1, :]
                later.append(c)
            rest = rest[SUB:, :]
            for j in range(SUB):
                rest = rest - lower[j] * tall(rows[j])
            column = later
        done = jnp.concatenate(finished, axis=0)
        done = jnp.where((lane < STEP) & (lane >= (row_in // (SPAN * SUB) + 1) * (SPAN * SUB)), 0.0, done)
        across = jnp.where((lane >= STEP) & (lane < width - s * STEP), done, 0.0)
        turned = pltpu.roll(done, width - STEP, 1)
        aug[: width - STEP, :] = below_rows - matmul(across.T[STEP:], turned)
        aug[width - STEP :, :] = turned
        return carry

    lax.fori_loop(0, width // STEP, step, 0)


def kernel(
    sizes, window, out, diag, across, panel, share, staged, aug, inverse, cross, rest, left, peer_ready, mate_ready,
    diag_send, diag_recv, pass_send, pass_recv, near_send, near_recv, across_send, across_recv, half_send, half_recv, panel_send,
    panel_recv, share_sem, out_sem,
):
    layers, grid_rows, grid_cols, row_blocks, col_blocks, width = sizes
    rows_here = width // layers
    half = width // 2
    split = 2 if grid_rows % 2 == 0 else 1
    skip = 1 if grid_rows <= PANELS else 0
    me_layer, me_row, me_col = lax.axis_index("layer"), lax.axis_index("row"), lax.axis_index("col")
    mine = lax.rem(me_row, split)
    pair = 2 if layers % 2 == 0 else 1
    odd = lax.rem(me_layer, pair)
    twin = (me_layer + 1 - 2 * odd, me_row, me_col)

    def at(layer, row, col):
        return (lax.rem(me_layer + layer, layers), lax.rem(me_row + row, grid_rows), lax.rem(me_col + col, grid_cols))

    def mate(layer, part):
        return (lax.rem(me_layer + layer, layers), me_row - mine + lax.rem(mine + part, split), me_col)

    def remote(src, dst, send, recv, target):
        return pltpu.make_async_remote_copy(
            src_ref=src, dst_ref=dst, send_sem=send, recv_sem=recv, device_id=target,
            device_id_type=pl.DeviceIdType.MESH,
        )

    def wait(ref, sem):
        pltpu.make_async_copy(ref, ref, sem).wait()

    here = pl.ds(pl.multiple_of(me_layer * rows_here, rows_here), rows_here)
    share_copies = [
        pltpu.make_async_copy(window.at[:, 0, here, slot, 0, :], share.at[slot], share_sem.at[slot])
        for slot in range(col_blocks)
    ]

    peers = [(row, col) for col in reversed(range(grid_cols)) for row in range(grid_rows) if row or col]
    mates = [(layer, part) for layer in reversed(range(layers)) for part in reversed(range(split)) if layer or part]
    diag[0, :half, half:] = jnp.zeros((half, width - half), jnp.float32)
    def signal(sem, target):
        pl.semaphore_signal(sem, inc=1, device_id=target, device_id_type=pl.DeviceIdType.MESH)

    def peer_after(row, col):
        _, other_row, other_col = at(0, row, col)
        return (other_col > me_col) | ((other_col == me_col) & (other_row > me_row))

    def mate_after(layer):
        return lax.rem(me_layer + layer, layers) > me_layer

    def owner(row, col):
        found = (row == PIECES[1][0]) & (col == PIECES[1][1])
        for i, j, *_ in PIECES[2:]:
            found = found | ((row == i) & (col == j))
        return found

    def known(row, col):
        return col == 0 or (row == 0 and col == 1)

    def talks(row, col, sender_row, sender_col):
        if known(row, col):
            return True
        return owner(sender_row, sender_col)

    far_mates = [(layer, part) for layer, part in mates if layer]
    barrier = pltpu.get_barrier_semaphore()
    for row, col in peers:
        @pl.when(peer_after(row, col))
        def _(row=row, col=col):
            signal(barrier, at(0, row, col))
    for layer, part in far_mates:
        @pl.when(mate_after(layer))
        def _(layer=layer, part=part):
            signal(barrier, mate(layer, part))
    before = me_col * grid_rows + me_row + me_layer * split

    @pl.when(before > 0)
    def _():
        pl.semaphore_wait(barrier, before)

    for row, col in peers:
        back = (-row % grid_rows, -col % grid_cols)
        _, to_row, to_col = at(0, row, col)

        @pl.when(jnp.logical_not(peer_after(row, col)) & talks(*back, to_row, to_col))
        def _(row=row, col=col, back=back):
            signal(peer_ready.at[back[0], back[1]], at(0, row, col))
    for layer, part in far_mates:
        @pl.when(jnp.logical_not(mate_after(layer)))
        def _(layer=layer, part=part):
            signal(mate_ready.at[-layer % layers, -part % split], mate(layer, part))

    def peer_entered(row, col):
        @pl.when(peer_after(row, col) & talks(row, col, me_row, me_col))
        def _():
            pl.semaphore_wait(peer_ready.at[row, col], 1)

    def mates_entered():
        for layer, part in far_mates:
            @pl.when(mate_after(layer))
            def _(layer=layer, part=part):
                pl.semaphore_wait(mate_ready.at[layer, part], 1)

    def peers_entered(mine_too):
        for row, col in peers:
            if known(row, col) == (not mine_too):
                peer_entered(row, col)

    def extent(p):
        _, _, slot, lower, side = PIECES[p]
        first, count = (0, width) if lower is None else (lower * half, half)
        return slot, first, count, pl.ds(0, width if side is None else half)

    def part_rows(p, part):
        _, first, count, _ = extent(p)
        size = count // (layers * split)
        return pl.ds(pl.multiple_of(first + (me_layer * split + part) * size, size), size)

    def diag_src(p, part):
        return window.at[0, 0, part_rows(p, part), 0, 0, extent(p)[3]]

    def diag_dst(p, part):
        return diag.at[extent(p)[0], part_rows(p, part), extent(p)[3]]

    def some(p, parts):
        slot, first, count, columns = extent(p)
        return diag.at[slot, pl.ds(first, parts * (count // (layers * split))), columns]

    def diag_copy(p, row, col):
        part = lax.rem(lax.rem(me_row + row, grid_rows), split)
        return remote(diag_src(p, part), diag_dst(p, part), diag_send.at[p, col], diag_recv.at[p], at(0, row, col))

    def diag_local(p):
        return pltpu.make_async_copy(diag_src(p, mine), diag_dst(p, mine), diag_recv.at[p])

    owners = [(me_row == piece[0]) & (me_col == piece[1]) for piece in PIECES]

    def whole(p):
        return PIECES[p][:2] == PIECES[0][:2]

    def here_whole(p):
        return me_col == PIECES[p][1]

    def full(ref, p):
        slot, first, count, columns = extent(p)
        return ref.at[0, 0, pl.ds(first, count), 0, 0, columns] if ref is window else ref.at[slot, pl.ds(first, count), columns]

    def diag_out(p):
        @pl.when(owners[p])
        def _():
            for col in range(grid_cols):
                for row in range(grid_rows):
                    if not (row or col):
                        continue
                    if col == 0 and whole(p):
                        remote(full(window, p), full(diag, p), diag_send.at[p, col], diag_recv.at[p], at(0, row, col)).start()
                    else:
                        if p == ORDER[0] and not known(row, col):
                            peer_entered(row, col)
                        diag_copy(p, row, col).start()
            if whole(p):
                pltpu.make_async_copy(full(window, p), full(diag, p), diag_recv.at[p]).start()
            else:
                diag_local(p).start()

    def targets(p):
        return [m for m in mates if p not in SHARED or pair == 1 or m[0] % pair == 0]

    def stripe_rows(p, layer):
        _, first, count, _ = extent(p)
        size = count // layers
        return pl.ds(pl.multiple_of(first + lax.rem(me_layer + layer, layers) * size, size), size)

    def shared(p):
        return p in SHARED and pair > 1

    def diag_pass(p):
        def run():
            wait(diag_dst(p, mine), diag_recv.at[p])
            for layer, part in targets(p):
                remote(diag_dst(p, mine), diag_dst(p, mine), pass_send.at[p], pass_recv.at[p], mate(layer, part)).start()

        if whole(p):
            pl.when(jnp.logical_not(here_whole(p)))(run)
        else:
            run()

    def diag_near(p):
        if shared(p):
            wait(some(p, len(targets(p))), pass_recv.at[p])
            for layer in range(0, layers, pair):
                part = diag.at[extent(p)[0], stripe_rows(p, layer), extent(p)[3]]
                remote(part, part, near_send.at[p], near_recv.at[p], twin).start()

    def diag_arrived(p):
        if shared(p):
            wait(some(p, layers * split // pair), near_recv.at[p])
        elif whole(p):
            @pl.when(here_whole(p))
            def _():
                wait(full(diag, p), diag_recv.at[p])

            @pl.when(jnp.logical_not(here_whole(p)))
            def _():
                wait(some(p, len(mates)), pass_recv.at[p])
        else:
            wait(some(p, len(mates)), pass_recv.at[p])

    def panel_src(i):
        return window.at[i, 0, here, 0, 0, :]

    def panel_hop(k, i, src, way):
        return remote(src, panel.at[k, i], panel_send.at[k, 0 if way < 0 else 1], panel_recv.at[k, i], (me_layer, me_row, me_col + way))

    chunks = range(skip, row_blocks)

    def up(k):
        return (me_col >= k) & (me_col < grid_cols - 1)

    def down(k):
        return (me_col <= k) & (me_col > 0)

    def panel_out(k, i, src):
        @pl.when(up(k))
        def _():
            panel_hop(k, i, src, 1).start()

        if k:
            @pl.when(down(k))
            def _():
                panel_hop(k, i, src, -1).start()

    def panel_begin():
        for k in range(PANELS):
            @pl.when(me_col == k)
            def _(k=k):
                for i in chunks:
                    panel_out(k, i, panel_src(i))
                    pltpu.make_async_copy(panel_src(i), panel.at[k, i], panel_recv.at[k, i]).start()

    def passes(k):
        return ((me_col > k) & (me_col < grid_cols - 1)) | ((me_col < k) & (me_col > 0))

    def panel_next(k, i, distance):
        @pl.when(passes(k) & (jnp.abs(me_col - k) == distance))
        def _():
            wait(panel.at[k, i], panel_recv.at[k, i])
            panel_out(k, i, panel.at[k, i])

    def panel_arrived(k, i):
        @pl.when(jnp.logical_not(passes(k)))
        def _():
            wait(panel.at[k, i], panel_recv.at[k, i])

    def some_rows(which):
        return pl.ds(pl.multiple_of(which * (width // pair), width // pair), width // pair)

    def across_copy(k, slot, n):
        return remote(
            window.at[0, 0, some_rows(odd), slot, 0, :], across.at[k, slot, some_rows(odd)], across_send.at[k, slot],
            across_recv.at[k, slot], at(0, n, 0),
        )

    def across_begin():
        for k in range(PANELS):
            @pl.when(me_row == k)
            def _(k=k):
                for slot in range(col_blocks):
                    for n in range(1, grid_rows):
                        across_copy(k, slot, n).start()
                    pltpu.make_async_copy(window.at[0, 0, :, slot, 0, :], across.at[k, slot], across_recv.at[k, slot]).start()

    def across_half(k, slot):
        return across.at[k, slot, some_rows(odd)]

    def across_near(slot):
        for k in range(PANELS):
            @pl.when(me_row != k)
            def _(k=k):
                wait(across_half(k, slot), across_recv.at[k, slot])
                if pair > 1:
                    remote(across_half(k, slot), across_half(k, slot), half_send.at[k, slot], half_recv.at[k, slot], twin).start()

    def across_arrived(k, slot):
        @pl.when(me_row == k)
        def _():
            wait(across.at[k, slot], across_recv.at[k, slot])

        if pair > 1:
            @pl.when(me_row != k)
            def _():
                wait(across_half(k, slot), half_recv.at[k, slot])

    steps = half // STEP
    plan = [[] for _ in range(4 * steps)]
    def mates_first():
        pl.when(here_whole(0))(mates_entered)

    plan[0].append(functools.partial(diag_pass, 1))
    plan[0].append(mates_first)
    plan[2].append(functools.partial(diag_pass, 2))
    plan[3].append(functools.partial(diag_pass, 3))
    plan[PANEL].append(panel_begin)
    plan[6].append(functools.partial(diag_near, 2))
    plan[ACROSS].append(across_begin)
    plan[7].append(functools.partial(diag_near, 3))
    plan[12].append(functools.partial(across_near, 0))
    plan[14].append(functools.partial(across_near, 1))
    final = []
    for distance in range(1, grid_cols):
        for i in chunks:
            for k in range(PANELS):
                when = HOP + HOPS * (distance - 1) + (i - skip)
                (plan[when] if when < 4 * steps else final).append(functools.partial(panel_next, k, i, distance))
    for i in chunks:
        for k in range(PANELS):
            final.append(functools.partial(panel_arrived, k, i))

    def hook(b):
        def run(s):
            for t in range(steps):
                if plan[b * steps + t]:
                    @pl.when(s == t)
                    def _(t=t):
                        for action in plan[b * steps + t]:
                            action()
        return run

    peers_entered(False)
    diag_out(ORDER[0])

    @pl.when(owner(me_row, me_col) & jnp.logical_not(owners[ORDER[0]]))
    def _():
        peers_entered(True)

    for p in ORDER[1:]:
        diag_out(p)

    @pl.when(jnp.logical_not(here_whole(0)))
    def _():
        mates_entered()

    diag_pass(0)
    for copy in share_copies:
        copy.start()
    diag_arrived(0)

    def inverted(b, value):
        aug[...] = value
        invert(aug, half, hook(b))
        return aug[...]

    def joined(k, first, second, below):
        inverse[k, :half, :half] = first
        inverse[k, :half, half:] = jnp.zeros((half, half), jnp.float32)
        inverse[k, half:, half:] = second
        inverse[k, half:, :half] = -matmul(second, matmul(below, first))

    inv0 = inverted(0, diag[0, :half, :half])
    inverse[0, :half, :half] = inv0
    diag_arrived(1)
    below0 = matmul_t(diag[0, half:, :half], inv0)
    cross[:half, :half] = below0
    inv1 = inverted(1, diag[0, half:, half:] - matmul_t(below0, below0))
    diag_arrived(2)
    below0, inv0 = cross[:half, :half], inverse[0, :half, :half]
    cross0 = matmul_t(diag[1, :, :half], inv0)
    cross1 = matmul_t(diag[1, :, half:] - matmul_t(cross0, below0), inv1)
    cross[:, :half] = cross0
    cross[:, half:] = cross1
    joined(0, inv0, inv1, below0)
    diag_arrived(3)
    rest[...] = diag[2] - matmul_t(cross0, cross0) - matmul_t(cross1, cross1)
    inv2 = inverted(2, rest[:half, :half])
    inverse[1, :half, :half] = inv2
    below1 = matmul_t(rest[half:, :half], inv2)
    left[0, :half, :half] = below1
    inv3 = inverted(3, rest[half:, half:] - matmul_t(below1, below1))
    joined(1, inverse[1, :half, :half], inv3, left[0, :half, :half])

    for action in final:
        action()
    kept = (row_blocks - skip) * rows_here
    left[0, : kept] = update(panel[0, skip:].reshape(kept, width), inverse[0], 1)
    left[1, : kept] = update(panel[1, skip:].reshape(kept, width) - update(left[0, :kept], cross[...], 1), inverse[1], 1)
    row = lax.broadcasted_iota(jnp.int32, (rows_here, width), 0) + me_layer * rows_here
    lower = row >= lax.broadcasted_iota(jnp.int32, (rows_here, width), 1)
    factor0 = jnp.where(lower, matmul_t(diag[0, here, :], inverse[0]), 0.0)
    factor1 = jnp.where(lower, matmul_t(rest[here, :], inverse[1]), 0.0)
    plain0 = cross[here, :] if skip else left[0, :rows_here]
    plain1 = factor1 if skip else left[1, :rows_here]
    first0 = jnp.where(me_row == 0, factor0, plain0)
    first1 = jnp.where(me_row == 0, 0.0, jnp.where(me_row == 1, factor1, plain1))

    def out_copy(slot):
        return pltpu.make_async_copy(staged.at[slot], out.at[:, 0, :, slot, 0, :], out_sem.at[slot])

    for slot in range(col_blocks):
        for k in range(PANELS):
            across_arrived(k, slot)
        share_copies[slot].wait()
        right0 = update(inverse[0], across[0, slot], 0)
        right1 = update(inverse[1], across[1, slot] - update(cross[...], right0, 0), 0)
        number = slot * grid_cols + me_col
        updated = share[slot, skip:].reshape(kept, width)
        updated -= update(left[0, :kept], right0, 0) + update(left[1, :kept], right1, 0)
        value = jnp.where(number == 0, left[0, :kept], jnp.where(number == 1, left[1, :kept], updated))
        staged[slot, skip:] = value.reshape(row_blocks - skip, rows_here, width)
        plain = 0.0 if skip else jnp.where(me_row < PANELS, 0.0, updated[:rows_here])
        staged[slot, 0] = jnp.where(number == 0, first0, jnp.where(number == 1, first1, plain))
        out_copy(slot).start()

    for p in range(len(PIECES)):
        @pl.when(owners[p])
        def _(p=p):
            for col in range(grid_cols):
                if col == 0 and whole(p):
                    for _ in range(1, grid_rows):
                        wait(full(diag, p), diag_send.at[p, col])
                else:
                    wait(some(p, grid_rows if col else grid_rows - 1), diag_send.at[p, col])

        def sent(p=p):
            wait(some(p, len(targets(p))), pass_send.at[p])

        if whole(p):
            pl.when(jnp.logical_not(here_whole(p)))(sent)
        else:
            sent()
        if shared(p):
            wait(some(p, layers * split // pair), near_send.at[p])
    for k in range(PANELS):
        @pl.when(up(k))
        def _(k=k):
            wait(panel.at[k, skip:], panel_send.at[k, 1])

        if k:
            @pl.when(down(k))
            def _(k=k):
                wait(panel.at[k, skip:], panel_send.at[k, 0])

        @pl.when(me_row == k)
        def _(k=k):
            for slot in range(col_blocks):
                for n in range(1, grid_rows):
                    wait(across_half(k, slot), across_send.at[k, slot])
    if pair > 1:
        for k in range(PANELS):
            @pl.when(me_row != k)
            def _(k=k):
                for slot in range(col_blocks):
                    wait(across_half(k, slot), half_send.at[k, slot])
    for slot in range(col_blocks):
        out_copy(slot).wait()


def local(sizes, schur_window):
    layers, grid_rows, grid_cols, row_blocks, col_blocks, width = sizes
    rows_here = width // layers
    anywhere = pl.BlockSpec(memory_space=pl.ANY)
    dma = pltpu.SemaphoreType.DMA
    pieces, diagonals, half = len(PIECES), len({p[2] for p in PIECES}), width // 2
    split = 2 if grid_rows % 2 == 0 else 1
    f32 = jnp.float32
    return pl.pallas_call(
        functools.partial(kernel, sizes),
        out_shape=jax.ShapeDtypeStruct((row_blocks, 1, rows_here, col_blocks, 1, width), f32),
        in_specs=[anywhere],
        out_specs=anywhere,
        scratch_shapes=[
            pltpu.VMEM((diagonals, width, width), f32),
            pltpu.VMEM((PANELS, col_blocks, width, width), f32),
            pltpu.VMEM((PANELS, row_blocks, rows_here, width), f32),
            pltpu.VMEM((col_blocks, row_blocks, rows_here, width), f32),
            pltpu.VMEM((col_blocks, row_blocks, rows_here, width), f32),
            pltpu.VMEM((half, half), f32),
            pltpu.VMEM((PANELS, width, width), f32),
            pltpu.VMEM((width, width), f32),
            pltpu.VMEM((width, width), f32),
            pltpu.VMEM((PANELS, row_blocks * rows_here, width), f32),
            pltpu.SemaphoreType.REGULAR((grid_rows, grid_cols)),
            pltpu.SemaphoreType.REGULAR((layers, split)),
            dma((pieces, grid_cols)),
            dma((pieces,)),
            dma((pieces,)),
            dma((pieces,)),
            dma((pieces,)),
            dma((pieces,)),
            dma((PANELS, col_blocks)),
            dma((PANELS, col_blocks)),
            dma((PANELS, col_blocks)),
            dma((PANELS, col_blocks)),
            dma((PANELS, 2)),
            dma((PANELS, row_blocks)),
            dma((col_blocks,)),
            dma((col_blocks,)),
        ],
        compiler_params=pltpu.CompilerParams(collective_id=0, has_side_effects=True),
        name="window",
    )(schur_window)


def solution(mesh):
    def body(schur_window):
        row_blocks, _, width, col_blocks, _, _ = schur_window.shape
        sizes = (mesh.shape["layer"], mesh.shape["row"], mesh.shape["col"], row_blocks, col_blocks, width)
        return local(sizes, schur_window)

    return jax.shard_map(
        body,
        mesh=mesh,
        in_specs=(P(None, "row", None, None, "col", None),),
        out_specs=P(None, "row", "layer", None, "col", None),
        check_vma=False,
    )
```

```python
import functools

import jax
import jax.numpy as jnp
from jax import lax
from jax.experimental import pallas as pl
from jax.experimental.pallas import tpu as pltpu
from jax.sharding import PartitionSpec as P

PANELS = 2
SUB = 8
LANES = 128
KEEP = 4
STEP = 32
SPAN = 2
SHARED = (2, 3)
ORDER = (0, 1, 2, 3)
PANEL = 2
ACROSS = 6
HOP = 7
HOPS = 3
PIECES = ((0, 0, 0, 0, 0), (0, 0, 0, 1, None), (1, 0, 1, None, None), (1, 1, 2, None, None))


def dot(a, b, lhs, rhs):
    return lax.dot_general(
        a, b, (((lhs,), (rhs,)), ((), ())),
        precision=lax.Precision.HIGHEST, preferred_element_type=jnp.float32,
    )


def matmul(a, b):
    return dot(a, b, 1, 0)


def matmul_t(a, b):
    return dot(a, b, 1, 1)


def update(a, b, rhs):
    a0, b0 = a.astype(jnp.bfloat16), b.astype(jnp.bfloat16)
    a1 = (a - a0.astype(jnp.float32)).astype(jnp.bfloat16)
    b1 = (b - b0.astype(jnp.float32)).astype(jnp.bfloat16)

    def product(x, y):
        return lax.dot_general(x, y, (((1,), (rhs,)), ((), ())), preferred_element_type=jnp.float32)

    return product(a0, b0) + (product(a0, b1) + product(a1, b0))


def spread(tile, start, count):
    size, lanes = tile.shape
    return [
        jnp.broadcast_to(tile[m // SUB * SUB :, start + m : start + m + 1], (size - m // SUB * SUB, lanes))
        for m in range(count)
    ]


def invert(aug, width, hook):
    sub = lax.broadcasted_iota(jnp.int32, (SUB, width), 0)
    lane = lax.broadcasted_iota(jnp.int32, (STEP, width), 1)
    row_in = lax.broadcasted_iota(jnp.int32, (STEP, width), 0)
    lane_below = lax.broadcasted_iota(jnp.int32, (width - STEP, width), 1)
    eye = jnp.where(lane == row_in, 1.0, 0.0).astype(jnp.float32)
    groups = STEP // SUB

    def step(s, carry):
        if hook is not None:
            hook(s)
        rest = aug[:STEP, :]
        below_rows = pltpu.roll(jnp.where(lane_below < STEP, 0.0, aug[STEP:, :]), width - STEP, 1)
        keep = row_in < STEP + s
        finished = []
        for g in range(groups):
            if g % SPAN == 0:
                column = spread(rest, g * SUB, SPAN * SUB)
                own = (lane >= g * SUB) & (lane < (g + SPAN) * SUB)
                rest = jnp.where(own[g * SUB :], eye[g * SUB :], rest)
                column = [jnp.where(keep[: c.shape[0]], c, 0.0) for c in column]
            rows = [jnp.broadcast_to(rest[j : j + 1, :], (SUB, width)) for j in range(SUB)]
            entry = [
                [jnp.broadcast_to(column[k][j : j + 1, :], (SUB, width)) if k >= j else None for k in range(SUB)]
                for j in range(SUB)
            ]
            done = jnp.zeros((SUB, width), jnp.float32)
            scales, lows = [], []
            for j in range(SUB):
                scale = lax.rsqrt(entry[j][j])
                rows[j] = rows[j] * scale
                done = jnp.where(sub == j, rows[j], done)
                low = [entry[j][k] * scale if k > j else None for k in range(SUB)]
                for k in range(j + 1, SUB):
                    for m in range(k, SUB):
                        entry[k][m] = entry[k][m] - low[k] * low[m]
                    rows[k] = rows[k] - low[k] * rows[j]
                scales.append(scale)
                lows.append(low)
            finished.append(done)
            after = groups - 1 - g
            if not after:
                break

            def tall(value):
                return jnp.concatenate([value] * after, axis=0) if after > 1 else value

            lower = []
            for j in range(SUB):
                c = column[j][SUB:, :]
                for i in range(j):
                    c = c - lower[i] * tall(lows[i][j])
                lower.append(c * tall(scales[j]))
            later = []
            for m in range(SUB, len(column)) if g % SPAN < SPAN - 1 else ():
                c = column[m]
                for j in range(SUB):
                    c = c - lower[j][m // SUB * SUB - SUB :, :] * lower[j][m - SUB : m - SUB + 1, :]
                later.append(c)
            rest = rest[SUB:, :]
            for j in range(SUB):
                rest = rest - lower[j] * tall(rows[j])
            column = later
        done = jnp.concatenate(finished, axis=0)
        done = jnp.where((lane < STEP) & (lane >= (row_in // (SPAN * SUB) + 1) * (SPAN * SUB)), 0.0, done)
        across = jnp.where((lane >= STEP) & (lane < width - s * STEP), done, 0.0)
        turned = pltpu.roll(done, width - STEP, 1)
        aug[: width - STEP, :] = below_rows - matmul(across.T[STEP:], turned)
        aug[width - STEP :, :] = turned
        return carry

    lax.fori_loop(0, width // STEP, step, 0)


def kernel(
    sizes, window, out, diag, across, panel, share, staged, aug, inverse, cross, rest, left, peer_ready, mate_ready,
    diag_send, diag_recv, pass_send, pass_recv, near_send, near_recv, across_send, across_recv, half_send, half_recv, panel_send,
    panel_recv, share_sem, out_sem,
):
    layers, grid_rows, grid_cols, row_blocks, col_blocks, width = sizes
    rows_here = width // layers
    half = width // 2
    split = 2 if grid_rows % 2 == 0 else 1
    skip = 1 if grid_rows <= PANELS else 0
    me_layer, me_row, me_col = lax.axis_index("layer"), lax.axis_index("row"), lax.axis_index("col")
    mine = lax.rem(me_row, split)
    pair = 2 if layers % 2 == 0 else 1
    odd = lax.rem(me_layer, pair)
    twin = (me_layer + 1 - 2 * odd, me_row, me_col)

    def at(layer, row, col):
        return (lax.rem(me_layer + layer, layers), lax.rem(me_row + row, grid_rows), lax.rem(me_col + col, grid_cols))

    def mate(layer, part):
        return (lax.rem(me_layer + layer, layers), me_row - mine + lax.rem(mine + part, split), me_col)

    def remote(src, dst, send, recv, target):
        return pltpu.make_async_remote_copy(
            src_ref=src, dst_ref=dst, send_sem=send, recv_sem=recv, device_id=target,
            device_id_type=pl.DeviceIdType.MESH,
        )

    def wait(ref, sem):
        pltpu.make_async_copy(ref, ref, sem).wait()

    here = pl.ds(pl.multiple_of(me_layer * rows_here, rows_here), rows_here)
    share_copies = [
        pltpu.make_async_copy(window.at[:, 0, here, slot, 0, :], share.at[slot], share_sem.at[slot])
        for slot in range(col_blocks)
    ]

    peers = [(row, col) for col in reversed(range(grid_cols)) for row in range(grid_rows) if row or col]
    mates = [(layer, part) for layer in reversed(range(layers)) for part in reversed(range(split)) if layer or part]
    diag[0, :half, half:] = jnp.zeros((half, width - half), jnp.float32)
    def signal(sem, target):
        pl.semaphore_signal(sem, inc=1, device_id=target, device_id_type=pl.DeviceIdType.MESH)

    def peer_after(row, col):
        _, other_row, other_col = at(0, row, col)
        return (other_col > me_col) | ((other_col == me_col) & (other_row > me_row))

    def mate_after(layer):
        return lax.rem(me_layer + layer, layers) > me_layer

    def owner(row, col):
        found = (row == PIECES[1][0]) & (col == PIECES[1][1])
        for i, j, *_ in PIECES[2:]:
            found = found | ((row == i) & (col == j))
        return found

    def known(row, col):
        return col == 0 or (row == 0 and col == 1)

    def talks(row, col, sender_row, sender_col):
        if known(row, col):
            return True
        return owner(sender_row, sender_col)

    far_mates = [(layer, part) for layer, part in mates if layer]
    barrier = pltpu.get_barrier_semaphore()
    for row, col in peers:
        @pl.when(peer_after(row, col))
        def _(row=row, col=col):
            signal(barrier, at(0, row, col))
    for layer, part in far_mates:
        @pl.when(mate_after(layer))
        def _(layer=layer, part=part):
            signal(barrier, mate(layer, part))
    before = me_col * grid_rows + me_row + me_layer * split

    @pl.when(before > 0)
    def _():
        pl.semaphore_wait(barrier, before)

    for row, col in peers:
        back = (-row % grid_rows, -col % grid_cols)
        _, to_row, to_col = at(0, row, col)

        @pl.when(jnp.logical_not(peer_after(row, col)) & talks(*back, to_row, to_col))
        def _(row=row, col=col, back=back):
            signal(peer_ready.at[back[0], back[1]], at(0, row, col))
    for layer, part in far_mates:
        @pl.when(jnp.logical_not(mate_after(layer)))
        def _(layer=layer, part=part):
            signal(mate_ready.at[-layer % layers, -part % split], mate(layer, part))

    def peer_entered(row, col):
        @pl.when(peer_after(row, col) & talks(row, col, me_row, me_col))
        def _():
            pl.semaphore_wait(peer_ready.at[row, col], 1)

    def mates_entered():
        for layer, part in far_mates:
            @pl.when(mate_after(layer))
            def _(layer=layer, part=part):
                pl.semaphore_wait(mate_ready.at[layer, part], 1)

    def peers_entered(mine_too):
        for row, col in peers:
            if known(row, col) == (not mine_too):
                peer_entered(row, col)

    def extent(p):
        _, _, slot, lower, side = PIECES[p]
        first, count = (0, width) if lower is None else (lower * half, half)
        return slot, first, count, pl.ds(0, width if side is None else half)

    def part_rows(p, part):
        _, first, count, _ = extent(p)
        size = count // (layers * split)
        return pl.ds(pl.multiple_of(first + (me_layer * split + part) * size, size), size)

    def diag_src(p, part):
        return window.at[0, 0, part_rows(p, part), 0, 0, extent(p)[3]]

    def diag_dst(p, part):
        return diag.at[extent(p)[0], part_rows(p, part), extent(p)[3]]

    def some(p, parts):
        slot, first, count, columns = extent(p)
        return diag.at[slot, pl.ds(first, parts * (count // (layers * split))), columns]

    def diag_copy(p, row, col):
        part = lax.rem(lax.rem(me_row + row, grid_rows), split)
        return remote(diag_src(p, part), diag_dst(p, part), diag_send.at[p, col], diag_recv.at[p], at(0, row, col))

    def diag_local(p):
        return pltpu.make_async_copy(diag_src(p, mine), diag_dst(p, mine), diag_recv.at[p])

    owners = [(me_row == piece[0]) & (me_col == piece[1]) for piece in PIECES]

    def whole(p):
        return PIECES[p][:2] == PIECES[0][:2]

    def here_whole(p):
        return me_col == PIECES[p][1]

    def full(ref, p):
        slot, first, count, columns = extent(p)
        return ref.at[0, 0, pl.ds(first, count), 0, 0, columns] if ref is window else ref.at[slot, pl.ds(first, count), columns]

    def diag_out(p):
        @pl.when(owners[p])
        def _():
            for col in range(grid_cols):
                for row in range(grid_rows):
                    if not (row or col):
                        continue
                    if col == 0 and whole(p):
                        remote(full(window, p), full(diag, p), diag_send.at[p, col], diag_recv.at[p], at(0, row, col)).start()
                    else:
                        if p == ORDER[0] and not known(row, col):
                            peer_entered(row, col)
                        diag_copy(p, row, col).start()
            if whole(p):
                pltpu.make_async_copy(full(window, p), full(diag, p), diag_recv.at[p]).start()
            else:
                diag_local(p).start()

    def targets(p):
        return [m for m in mates if p not in SHARED or pair == 1 or m[0] % pair == 0]

    def stripe_rows(p, layer):
        _, first, count, _ = extent(p)
        size = count // layers
        return pl.ds(pl.multiple_of(first + lax.rem(me_layer + layer, layers) * size, size), size)

    def shared(p):
        return p in SHARED and pair > 1

    def diag_pass(p):
        def run():
            wait(diag_dst(p, mine), diag_recv.at[p])
            for layer, part in targets(p):
                remote(diag_dst(p, mine), diag_dst(p, mine), pass_send.at[p], pass_recv.at[p], mate(layer, part)).start()

        if whole(p):
            pl.when(jnp.logical_not(here_whole(p)))(run)
        else:
            run()

    def diag_near(p):
        if shared(p):
            wait(some(p, len(targets(p))), pass_recv.at[p])
            for layer in range(0, layers, pair):
                part = diag.at[extent(p)[0], stripe_rows(p, layer), extent(p)[3]]
                remote(part, part, near_send.at[p], near_recv.at[p], twin).start()

    def diag_arrived(p):
        if shared(p):
            wait(some(p, layers * split // pair), near_recv.at[p])
        elif whole(p):
            @pl.when(here_whole(p))
            def _():
                wait(full(diag, p), diag_recv.at[p])

            @pl.when(jnp.logical_not(here_whole(p)))
            def _():
                wait(some(p, len(mates)), pass_recv.at[p])
        else:
            wait(some(p, len(mates)), pass_recv.at[p])

    def panel_src(i):
        return window.at[i, 0, here, 0, 0, :]

    def panel_hop(k, i, src, way):
        return remote(src, panel.at[k, i], panel_send.at[k, 0 if way < 0 else 1], panel_recv.at[k, i], (me_layer, me_row, me_col + way))

    chunks = range(skip, row_blocks)

    def up(k):
        return (me_col >= k) & (me_col < grid_cols - 1)

    def down(k):
        return (me_col <= k) & (me_col > 0)

    def panel_out(k, i, src):
        @pl.when(up(k))
        def _():
            panel_hop(k, i, src, 1).start()

        if k:
            @pl.when(down(k))
            def _():
                panel_hop(k, i, src, -1).start()

    def panel_begin():
        for k in range(PANELS):
            @pl.when(me_col == k)
            def _(k=k):
                for i in chunks:
                    panel_out(k, i, panel_src(i))
                    pltpu.make_async_copy(panel_src(i), panel.at[k, i], panel_recv.at[k, i]).start()

    def passes(k):
        return ((me_col > k) & (me_col < grid_cols - 1)) | ((me_col < k) & (me_col > 0))

    def panel_next(k, i, distance):
        @pl.when(passes(k) & (jnp.abs(me_col - k) == distance))
        def _():
            wait(panel.at[k, i], panel_recv.at[k, i])
            panel_out(k, i, panel.at[k, i])

    def panel_arrived(k, i):
        @pl.when(jnp.logical_not(passes(k)))
        def _():
            wait(panel.at[k, i], panel_recv.at[k, i])

    def some_rows(which):
        return pl.ds(pl.multiple_of(which * (width // pair), width // pair), width // pair)

    def across_copy(k, slot, n):
        return remote(
            window.at[0, 0, some_rows(odd), slot, 0, :], across.at[k, slot, some_rows(odd)], across_send.at[k, slot],
            across_recv.at[k, slot], at(0, n, 0),
        )

    def across_begin():
        for k in range(PANELS):
            @pl.when(me_row == k)
            def _(k=k):
                for slot in range(col_blocks):
                    for n in range(1, grid_rows):
                        across_copy(k, slot, n).start()
                    pltpu.make_async_copy(window.at[0, 0, :, slot, 0, :], across.at[k, slot], across_recv.at[k, slot]).start()

    def across_half(k, slot):
        return across.at[k, slot, some_rows(odd)]

    def across_near(slot):
        for k in range(PANELS):
            @pl.when(me_row != k)
            def _(k=k):
                wait(across_half(k, slot), across_recv.at[k, slot])
                if pair > 1:
                    remote(across_half(k, slot), across_half(k, slot), half_send.at[k, slot], half_recv.at[k, slot], twin).start()

    def across_arrived(k, slot):
        @pl.when(me_row == k)
        def _():
            wait(across.at[k, slot], across_recv.at[k, slot])

        if pair > 1:
            @pl.when(me_row != k)
            def _():
                wait(across_half(k, slot), half_recv.at[k, slot])

    steps = half // STEP
    plan = [[] for _ in range(4 * steps)]
    def mates_first():
        pl.when(here_whole(0))(mates_entered)

    plan[0].append(functools.partial(diag_pass, 1))
    plan[0].append(mates_first)
    plan[2].append(functools.partial(diag_pass, 2))
    plan[3].append(functools.partial(diag_pass, 3))
    plan[PANEL].append(panel_begin)
    plan[6].append(functools.partial(diag_near, 2))
    plan[ACROSS].append(across_begin)
    plan[7].append(functools.partial(diag_near, 3))
    plan[12].append(functools.partial(across_near, 0))
    plan[14].append(functools.partial(across_near, 1))
    final = []
    for distance in range(1, grid_cols):
        for i in chunks:
            for k in range(PANELS):
                when = HOP + HOPS * (distance - 1) + (i - skip)
                (plan[when] if when < 4 * steps else final).append(functools.partial(panel_next, k, i, distance))
    for i in chunks:
        for k in range(PANELS):
            final.append(functools.partial(panel_arrived, k, i))

    def hook(b):
        def run(s):
            for t in range(steps):
                if plan[b * steps + t]:
                    @pl.when(s == t)
                    def _(t=t):
                        for action in plan[b * steps + t]:
                            action()
        return run

    peers_entered(False)
    diag_out(ORDER[0])

    @pl.when(owner(me_row, me_col) & jnp.logical_not(owners[ORDER[0]]))
    def _():
        peers_entered(True)

    for p in ORDER[1:]:
        diag_out(p)

    @pl.when(jnp.logical_not(here_whole(0)))
    def _():
        mates_entered()

    diag_pass(0)
    for copy in share_copies:
        copy.start()
    diag_arrived(0)

    def inverted(b, value):
        aug[...] = value
        invert(aug, half, hook(b))
        return aug[...]

    def joined(k, first, second, below):
        inverse[k, :half, :half] = first
        inverse[k, :half, half:] = jnp.zeros((half, half), jnp.float32)
        inverse[k, half:, half:] = second
        inverse[k, half:, :half] = -update(second, update(below, first, 0), 0)

    inv0 = inverted(0, diag[0, :half, :half])
    inverse[0, :half, :half] = inv0
    diag_arrived(1)
    below0 = matmul_t(diag[0, half:, :half], inv0)
    cross[:half, :half] = below0
    inv1 = inverted(1, diag[0, half:, half:] - matmul_t(below0, below0))
    diag_arrived(2)
    below0, inv0 = cross[:half, :half], inverse[0, :half, :half]
    cross0 = matmul_t(diag[1, :, :half], inv0)
    cross1 = matmul_t(diag[1, :, half:] - matmul_t(cross0, below0), inv1)
    cross[:, :half] = cross0
    cross[:, half:] = cross1
    joined(0, inv0, inv1, below0)
    diag_arrived(3)
    rest[...] = diag[2] - matmul_t(cross0, cross0) - matmul_t(cross1, cross1)
    inv2 = inverted(2, rest[:half, :half])
    inverse[1, :half, :half] = inv2
    below1 = matmul_t(rest[half:, :half], inv2)
    left[0, :half, :half] = below1
    inv3 = inverted(3, rest[half:, half:] - matmul_t(below1, below1))
    joined(1, inverse[1, :half, :half], inv3, left[0, :half, :half])

    for action in final:
        action()
    kept = (row_blocks - skip) * rows_here
    left[0, : kept] = update(panel[0, skip:].reshape(kept, width), inverse[0], 1)
    left[1, : kept] = update(panel[1, skip:].reshape(kept, width) - update(left[0, :kept], cross[...], 1), inverse[1], 1)
    row = lax.broadcasted_iota(jnp.int32, (rows_here, width), 0) + me_layer * rows_here
    lower = row >= lax.broadcasted_iota(jnp.int32, (rows_here, width), 1)
    factor0 = jnp.where(lower, update(diag[0, here, :], inverse[0], 1), 0.0)
    factor1 = jnp.where(lower, update(rest[here, :], inverse[1], 1), 0.0)
    plain0 = cross[here, :] if skip else left[0, :rows_here]
    plain1 = factor1 if skip else left[1, :rows_here]
    first0 = jnp.where(me_row == 0, factor0, plain0)
    first1 = jnp.where(me_row == 0, 0.0, jnp.where(me_row == 1, factor1, plain1))

    def out_copy(slot):
        return [
            pltpu.make_async_copy(
                staged.at[slot, :, :, pl.ds(part * LANES, LANES)], out.at[:, :, slot * (width // LANES) + part, :], out_sem.at[slot, part]
            )
            for part in range(width // LANES)
        ]

    for slot in range(col_blocks):
        for k in range(PANELS):
            across_arrived(k, slot)
        share_copies[slot].wait()
        right0 = update(inverse[0], across[0, slot], 0)
        right1 = update(inverse[1], across[1, slot] - update(cross[...], right0, 0), 0)
        number = slot * grid_cols + me_col
        updated = share[slot, skip:].reshape(kept, width)
        updated -= update(left[0, :kept], right0, 0) + update(left[1, :kept], right1, 0)
        value = jnp.where(number == 0, left[0, :kept], jnp.where(number == 1, left[1, :kept], updated))
        staged[slot, skip:] = value.reshape(row_blocks - skip, rows_here, width)
        plain = 0.0 if skip else jnp.where(me_row < PANELS, 0.0, updated[:rows_here])
        staged[slot, 0] = jnp.where(number == 0, first0, jnp.where(number == 1, first1, plain))
        for copy in out_copy(slot):
            copy.start()

    for p in range(len(PIECES)):
        @pl.when(owners[p])
        def _(p=p):
            for col in range(grid_cols):
                if col == 0 and whole(p):
                    for _ in range(1, grid_rows):
                        wait(full(diag, p), diag_send.at[p, col])
                else:
                    wait(some(p, grid_rows if col else grid_rows - 1), diag_send.at[p, col])

        def sent(p=p):
            wait(some(p, len(targets(p))), pass_send.at[p])

        if whole(p):
            pl.when(jnp.logical_not(here_whole(p)))(sent)
        else:
            sent()
        if shared(p):
            wait(some(p, layers * split // pair), near_send.at[p])
    for k in range(PANELS):
        @pl.when(up(k))
        def _(k=k):
            wait(panel.at[k, skip:], panel_send.at[k, 1])

        if k:
            @pl.when(down(k))
            def _(k=k):
                wait(panel.at[k, skip:], panel_send.at[k, 0])

        @pl.when(me_row == k)
        def _(k=k):
            for slot in range(col_blocks):
                for n in range(1, grid_rows):
                    wait(across_half(k, slot), across_send.at[k, slot])
    if pair > 1:
        for k in range(PANELS):
            @pl.when(me_row != k)
            def _(k=k):
                for slot in range(col_blocks):
                    wait(across_half(k, slot), half_send.at[k, slot])
    for slot in range(col_blocks):
        for copy in out_copy(slot):
            copy.wait()


def keep(source, target, held, in_sem, out_sem):
    rows = source.shape[0] // KEEP
    parts = [pl.ds(n * rows, rows) for n in range(KEEP)]
    arrive = [pltpu.make_async_copy(source.at[part], held.at[part], in_sem.at[n]) for n, part in enumerate(parts)]
    leave = [pltpu.make_async_copy(held.at[part], target.at[part], out_sem.at[n]) for n, part in enumerate(parts)]
    for copy in arrive:
        copy.start()
    for n, copy in enumerate(leave):
        arrive[n].wait()
        copy.start()
    for copy in leave:
        copy.wait()


def local(sizes, schur_window):
    layers, grid_rows, grid_cols, row_blocks, col_blocks, width = sizes
    rows_here = width // layers
    anywhere = pl.BlockSpec(memory_space=pl.ANY)
    dma = pltpu.SemaphoreType.DMA
    pieces, diagonals, half = len(PIECES), len({p[2] for p in PIECES}), width // 2
    split = 2 if grid_rows % 2 == 0 else 1
    f32 = jnp.float32
    result = pl.pallas_call(
        functools.partial(kernel, sizes),
        out_shape=jax.ShapeDtypeStruct((row_blocks, rows_here, col_blocks * width // LANES, LANES), f32),
        in_specs=[anywhere],
        out_specs=anywhere,
        scratch_shapes=[
            pltpu.VMEM((diagonals, width, width), f32),
            pltpu.VMEM((PANELS, col_blocks, width, width), f32),
            pltpu.VMEM((PANELS, row_blocks, rows_here, width), f32),
            pltpu.VMEM((col_blocks, row_blocks, rows_here, width), f32),
            pltpu.VMEM((col_blocks, row_blocks, rows_here, width), f32),
            pltpu.VMEM((half, half), f32),
            pltpu.VMEM((PANELS, width, width), f32),
            pltpu.VMEM((width, width), f32),
            pltpu.VMEM((width, width), f32),
            pltpu.VMEM((PANELS, row_blocks * rows_here, width), f32),
            pltpu.SemaphoreType.REGULAR((grid_rows, grid_cols)),
            pltpu.SemaphoreType.REGULAR((layers, split)),
            dma((pieces, grid_cols)),
            dma((pieces,)),
            dma((pieces,)),
            dma((pieces,)),
            dma((pieces,)),
            dma((pieces,)),
            dma((PANELS, col_blocks)),
            dma((PANELS, col_blocks)),
            dma((PANELS, col_blocks)),
            dma((PANELS, col_blocks)),
            dma((PANELS, 2)),
            dma((PANELS, row_blocks)),
            dma((col_blocks,)),
            dma((col_blocks, width // LANES)),
        ],
        compiler_params=pltpu.CompilerParams(collective_id=0, has_side_effects=True),
        name="window",
    )(schur_window).reshape(-1, LANES)
    result = pl.pallas_call(
        keep, out_shape=jax.ShapeDtypeStruct(result.shape, f32), in_specs=[anywhere], out_specs=anywhere,
        scratch_shapes=[pltpu.VMEM(result.shape, f32), dma((KEEP,)), dma((KEEP,))], name="keep",
    )(result)
    return result.reshape(row_blocks, 1, rows_here, col_blocks, 1, width)


def solution(mesh):
    def body(schur_window):
        row_blocks, _, width, col_blocks, _, _ = schur_window.shape
        sizes = (mesh.shape["layer"], mesh.shape["row"], mesh.shape["col"], row_blocks, col_blocks, width)
        return local(sizes, schur_window)

    return jax.shard_map(
        body,
        mesh=mesh,
        in_specs=(P(None, "row", None, None, "col", None),),
        out_specs=P(None, "row", "layer", None, "col", None),
        check_vma=False,
    )
```

```python
import functools

import jax
import jax.numpy as jnp
from jax import lax
from jax.experimental import pallas as pl
from jax.experimental.pallas import tpu as pltpu
from jax.sharding import PartitionSpec as P

PANELS = 2
SUB = 8
LANES = 128
KEEP = 4
STEP = 32
SPAN = 2
SHARED = (2, 3)
ORDER = (0, 1, 2, 3)
PANEL = 2
ACROSS = 6
HOP = 7
HOPS = 3
PIECES = ((0, 0, 0, 0, 0), (0, 0, 0, 1, None), (1, 0, 1, None, None), (1, 1, 2, None, None))


def dot(a, b, lhs, rhs):
    return lax.dot_general(
        a, b, (((lhs,), (rhs,)), ((), ())),
        precision=lax.Precision.HIGHEST, preferred_element_type=jnp.float32,
    )


def matmul(a, b):
    return dot(a, b, 1, 0)


def matmul_t(a, b):
    return dot(a, b, 1, 1)


def update(a, b, rhs):
    a0, b0 = a.astype(jnp.bfloat16), b.astype(jnp.bfloat16)
    a1 = (a - a0.astype(jnp.float32)).astype(jnp.bfloat16)
    b1 = (b - b0.astype(jnp.float32)).astype(jnp.bfloat16)

    def product(x, y):
        return lax.dot_general(x, y, (((1,), (rhs,)), ((), ())), preferred_element_type=jnp.float32)

    return product(a0, b0) + (product(a0, b1) + product(a1, b0))


def spread(tile, start, count):
    size, lanes = tile.shape
    return [
        jnp.broadcast_to(tile[m // SUB * SUB :, start + m : start + m + 1], (size - m // SUB * SUB, lanes))
        for m in range(count)
    ]


def invert(aug, width, hook):
    sub = lax.broadcasted_iota(jnp.int32, (SUB, width), 0)
    lane = lax.broadcasted_iota(jnp.int32, (STEP, width), 1)
    row_in = lax.broadcasted_iota(jnp.int32, (STEP, width), 0)
    lane_below = lax.broadcasted_iota(jnp.int32, (width - STEP, width), 1)
    eye = jnp.where(lane == row_in, 1.0, 0.0).astype(jnp.float32)
    groups = STEP // SUB

    def step(s, carry):
        if hook is not None:
            hook(s)
        rest = aug[:STEP, :]
        below_rows = pltpu.roll(jnp.where(lane_below < STEP, 0.0, aug[STEP:, :]), width - STEP, 1)
        keep = row_in < STEP + s
        finished = []
        for g in range(groups):
            if g % SPAN == 0:
                column = spread(rest, g * SUB, SPAN * SUB)
                own = (lane >= g * SUB) & (lane < (g + SPAN) * SUB)
                rest = jnp.where(own[g * SUB :], eye[g * SUB :], rest)
            rows = [jnp.broadcast_to(rest[j : j + 1, :], (SUB, width)) for j in range(SUB)]
            square = [c[:SUB] if g % SPAN else jnp.where(keep[:SUB], c[:SUB], 0.0) for c in column[:SUB]]
            entry = [
                [jnp.broadcast_to(square[k][j : j + 1, :], (SUB, width)) if k >= j else None for k in range(SUB)]
                for j in range(SUB)
            ]
            done = jnp.zeros((SUB, width), jnp.float32)
            scales, lows = [], []
            for j in range(SUB):
                scale = lax.rsqrt(entry[j][j])
                rows[j] = rows[j] * scale
                done = jnp.where(sub == j, rows[j], done)
                low = [entry[j][k] * scale if k > j else None for k in range(SUB)]
                for k in range(j + 1, SUB):
                    for m in range(k, SUB):
                        entry[k][m] = entry[k][m] - low[k] * low[m]
                    rows[k] = rows[k] - low[k] * rows[j]
                scales.append(scale)
                lows.append(low)
            finished.append(done)
            after = groups - 1 - g
            if not after:
                break

            def tall(value):
                return jnp.concatenate([value] * after, axis=0) if after > 1 else value

            lower = []
            for j in range(SUB):
                c = column[j][SUB:, :]
                for i in range(j):
                    c = c - lower[i] * tall(lows[i][j])
                lower.append(c * tall(scales[j]))
            later = []
            for m in range(SUB, len(column)) if g % SPAN < SPAN - 1 else ():
                c = column[m]
                for j in range(SUB):
                    c = c - lower[j][m // SUB * SUB - SUB :, :] * lower[j][m - SUB : m - SUB + 1, :]
                later.append(c)
            rest = rest[SUB:, :]
            for j in range(SUB):
                rest = rest - lower[j] * tall(rows[j])
            column = later
        done = jnp.concatenate(finished, axis=0)
        done = jnp.where((lane < STEP) & (lane >= (row_in // (SPAN * SUB) + 1) * (SPAN * SUB)), 0.0, done)
        across = jnp.where((lane >= STEP) & (lane < width - s * STEP), done, 0.0)
        turned = pltpu.roll(done, width - STEP, 1)
        aug[: width - STEP, :] = below_rows - matmul(across.T[STEP:], turned)
        aug[width - STEP :, :] = turned
        return carry

    lax.fori_loop(0, width // STEP, step, 0)


def kernel(
    sizes, window, out, diag, across, panel, share, staged, aug, inverse, cross, rest, left, peer_ready, mate_ready,
    diag_send, diag_recv, pass_send, pass_recv, near_send, near_recv, across_send, across_recv, half_send, half_recv, panel_send,
    panel_recv, share_sem, out_sem,
):
    layers, grid_rows, grid_cols, row_blocks, col_blocks, width = sizes
    rows_here = width // layers
    half = width // 2
    split = 2 if grid_rows % 2 == 0 else 1
    skip = 1 if grid_rows <= PANELS else 0
    me_layer, me_row, me_col = lax.axis_index("layer"), lax.axis_index("row"), lax.axis_index("col")
    mine = lax.rem(me_row, split)
    pair = 2 if layers % 2 == 0 else 1
    odd = lax.rem(me_layer, pair)
    twin = (me_layer + 1 - 2 * odd, me_row, me_col)

    def at(layer, row, col):
        return (lax.rem(me_layer + layer, layers), lax.rem(me_row + row, grid_rows), lax.rem(me_col + col, grid_cols))

    def mate(layer, part):
        return (lax.rem(me_layer + layer, layers), me_row - mine + lax.rem(mine + part, split), me_col)

    def remote(src, dst, send, recv, target):
        return pltpu.make_async_remote_copy(
            src_ref=src, dst_ref=dst, send_sem=send, recv_sem=recv, device_id=target,
            device_id_type=pl.DeviceIdType.MESH,
        )

    def wait(ref, sem):
        pltpu.make_async_copy(ref, ref, sem).wait()

    here = pl.ds(pl.multiple_of(me_layer * rows_here, rows_here), rows_here)
    share_copies = [
        pltpu.make_async_copy(window.at[:, 0, here, slot, 0, :], share.at[slot], share_sem.at[slot])
        for slot in range(col_blocks)
    ]

    peers = [(row, col) for col in reversed(range(grid_cols)) for row in range(grid_rows) if row or col]
    mates = [(layer, part) for layer in reversed(range(layers)) for part in reversed(range(split)) if layer or part]
    def signal(sem, target):
        pl.semaphore_signal(sem, inc=1, device_id=target, device_id_type=pl.DeviceIdType.MESH)

    def peer_after(row, col):
        _, other_row, other_col = at(0, row, col)
        return (other_col > me_col) | ((other_col == me_col) & (other_row > me_row))

    def mate_after(layer):
        return lax.rem(me_layer + layer, layers) > me_layer

    def owner(row, col):
        found = (row == PIECES[1][0]) & (col == PIECES[1][1])
        for i, j, *_ in PIECES[2:]:
            found = found | ((row == i) & (col == j))
        return found

    def known(row, col):
        return col == 0 or (row == 0 and col == 1)

    def talks(row, col, sender_row, sender_col):
        if known(row, col):
            return True
        return owner(sender_row, sender_col)

    far_mates = [(layer, part) for layer, part in mates if layer]
    barrier = pltpu.get_barrier_semaphore()
    for row, col in peers:
        @pl.when(peer_after(row, col))
        def _(row=row, col=col):
            signal(barrier, at(0, row, col))
    for layer, part in far_mates:
        @pl.when(mate_after(layer))
        def _(layer=layer, part=part):
            signal(barrier, mate(layer, part))
    before = me_col * grid_rows + me_row + me_layer * split

    @pl.when(before > 0)
    def _():
        pl.semaphore_wait(barrier, before)

    for row, col in sorted(peers, key=lambda peer: (peer[1] - 1) % grid_cols):
        back = (-row % grid_rows, -col % grid_cols)
        _, to_row, to_col = at(0, row, col)

        @pl.when(jnp.logical_not(peer_after(row, col)) & talks(*back, to_row, to_col))
        def _(row=row, col=col, back=back):
            signal(peer_ready.at[back[0], back[1]], at(0, row, col))
    for layer, part in far_mates:
        @pl.when(jnp.logical_not(mate_after(layer)))
        def _(layer=layer, part=part):
            signal(mate_ready.at[-layer % layers, -part % split], mate(layer, part))

    def peer_entered(row, col):
        @pl.when(peer_after(row, col) & talks(row, col, me_row, me_col))
        def _():
            pl.semaphore_wait(peer_ready.at[row, col], 1)

    def mates_entered():
        for layer, part in far_mates:
            @pl.when(mate_after(layer))
            def _(layer=layer, part=part):
                pl.semaphore_wait(mate_ready.at[layer, part], 1)

    def peers_entered(mine_too):
        for row, col in peers:
            if known(row, col) == (not mine_too):
                peer_entered(row, col)

    def extent(p):
        _, _, slot, lower, side = PIECES[p]
        first, count = (0, width) if lower is None else (lower * half, half)
        return slot, first, count, pl.ds(0, width if side is None else half)

    def part_rows(p, part):
        _, first, count, _ = extent(p)
        size = count // (layers * split)
        return pl.ds(pl.multiple_of(first + (me_layer * split + part) * size, size), size)

    def diag_src(p, part):
        return window.at[0, 0, part_rows(p, part), 0, 0, extent(p)[3]]

    def diag_dst(p, part):
        return diag.at[extent(p)[0], part_rows(p, part), extent(p)[3]]

    def some(p, parts):
        slot, first, count, columns = extent(p)
        return diag.at[slot, pl.ds(first, parts * (count // (layers * split))), columns]

    def diag_copy(p, row, col):
        part = lax.rem(lax.rem(me_row + row, grid_rows), split)
        return remote(diag_src(p, part), diag_dst(p, part), diag_send.at[p, col], diag_recv.at[p], at(0, row, col))

    def diag_local(p):
        return pltpu.make_async_copy(diag_src(p, mine), diag_dst(p, mine), diag_recv.at[p])

    owners = [(me_row == piece[0]) & (me_col == piece[1]) for piece in PIECES]

    def whole(p):
        return PIECES[p][:2] == PIECES[0][:2]

    def here_whole(p):
        return me_col == PIECES[p][1]

    def full(ref, p):
        slot, first, count, columns = extent(p)
        return ref.at[0, 0, pl.ds(first, count), 0, 0, columns] if ref is window else ref.at[slot, pl.ds(first, count), columns]

    def diag_out(p):
        @pl.when(owners[p])
        def _():
            for col in range(grid_cols):
                for row in range(grid_rows):
                    if not (row or col):
                        continue
                    if col == 0 and whole(p):
                        remote(full(window, p), full(diag, p), diag_send.at[p, col], diag_recv.at[p], at(0, row, col)).start()
                    else:
                        if p == ORDER[0] and not known(row, col):
                            peer_entered(row, col)
                        diag_copy(p, row, col).start()
            if whole(p):
                pltpu.make_async_copy(full(window, p), full(diag, p), diag_recv.at[p]).start()
            else:
                diag_local(p).start()

    def targets(p):
        return [m for m in mates if p not in SHARED or pair == 1 or m[0] % pair == 0]

    def stripe_rows(p, layer):
        _, first, count, _ = extent(p)
        size = count // layers
        return pl.ds(pl.multiple_of(first + lax.rem(me_layer + layer, layers) * size, size), size)

    def shared(p):
        return p in SHARED and pair > 1

    def diag_pass(p):
        def run():
            wait(diag_dst(p, mine), diag_recv.at[p])
            for layer, part in targets(p):
                remote(diag_dst(p, mine), diag_dst(p, mine), pass_send.at[p], pass_recv.at[p], mate(layer, part)).start()

        if whole(p):
            pl.when(jnp.logical_not(here_whole(p)))(run)
        else:
            run()

    def diag_near(p):
        if shared(p):
            wait(some(p, len(targets(p))), pass_recv.at[p])
            for layer in range(0, layers, pair):
                part = diag.at[extent(p)[0], stripe_rows(p, layer), extent(p)[3]]
                remote(part, part, near_send.at[SHARED.index(p)], near_recv.at[SHARED.index(p)], twin).start()

    def diag_arrived(p):
        if shared(p):
            wait(some(p, layers * split // pair), near_recv.at[SHARED.index(p)])
        elif whole(p):
            @pl.when(here_whole(p))
            def _():
                wait(full(diag, p), diag_recv.at[p])

            @pl.when(jnp.logical_not(here_whole(p)))
            def _():
                wait(some(p, len(mates)), pass_recv.at[p])
        else:
            wait(some(p, len(mates)), pass_recv.at[p])

    def panel_src(i):
        return window.at[i, 0, here, 0, 0, :]

    def panel_hop(k, i, src, way):
        return remote(src, panel.at[k, i], panel_send.at[k, 0 if way < 0 else 1], panel_recv.at[k, i], (me_layer, me_row, me_col + way))

    chunks = range(skip, row_blocks)

    def up(k):
        return (me_col >= k) & (me_col < grid_cols - 1)

    def down(k):
        return (me_col <= k) & (me_col > 0)

    def panel_out(k, i, src):
        @pl.when(up(k))
        def _():
            panel_hop(k, i, src, 1).start()

        if k:
            @pl.when(down(k))
            def _():
                panel_hop(k, i, src, -1).start()

    def panel_begin():
        for k in range(PANELS):
            @pl.when(me_col == k)
            def _(k=k):
                for i in chunks:
                    panel_out(k, i, panel_src(i))
                    pltpu.make_async_copy(panel_src(i), panel.at[k, i], panel_recv.at[k, i]).start()

    def passes(k):
        return ((me_col > k) & (me_col < grid_cols - 1)) | ((me_col < k) & (me_col > 0))

    def panel_next(k, i, distance):
        @pl.when(passes(k) & (jnp.abs(me_col - k) == distance))
        def _():
            wait(panel.at[k, i], panel_recv.at[k, i])
            panel_out(k, i, panel.at[k, i])

    def panel_arrived(k, i):
        @pl.when(jnp.logical_not(passes(k)))
        def _():
            wait(panel.at[k, i], panel_recv.at[k, i])

    def some_rows(which):
        return pl.ds(pl.multiple_of(which * (width // pair), width // pair), width // pair)

    def across_copy(k, slot, n):
        return remote(
            window.at[0, 0, some_rows(odd), slot, 0, :], across.at[k, slot, some_rows(odd)], across_send.at[k, slot],
            across_recv.at[k, slot], at(0, n, 0),
        )

    def across_begin():
        for k in range(PANELS):
            @pl.when(me_row == k)
            def _(k=k):
                for slot in range(col_blocks):
                    for n in range(1, grid_rows):
                        across_copy(k, slot, n).start()
                    pltpu.make_async_copy(window.at[0, 0, :, slot, 0, :], across.at[k, slot], across_recv.at[k, slot]).start()

    def across_half(k, slot):
        return across.at[k, slot, some_rows(odd)]

    def across_near(slot):
        for k in range(PANELS):
            @pl.when(me_row != k)
            def _(k=k):
                wait(across_half(k, slot), across_recv.at[k, slot])
                if pair > 1:
                    remote(across_half(k, slot), across_half(k, slot), half_send.at[k, slot], half_recv.at[k, slot], twin).start()

    def across_arrived(k, slot):
        @pl.when(me_row == k)
        def _():
            wait(across.at[k, slot], across_recv.at[k, slot])

        if pair > 1:
            @pl.when(me_row != k)
            def _():
                wait(across_half(k, slot), half_recv.at[k, slot])

    steps = half // STEP
    plan = [[] for _ in range(4 * steps)]
    def mates_first():
        pl.when(here_whole(0))(mates_entered)

    plan[0].append(functools.partial(diag_pass, 1))
    plan[0].append(mates_first)
    plan[2].append(functools.partial(diag_pass, 2))
    plan[3].append(functools.partial(diag_pass, 3))
    plan[PANEL].append(panel_begin)
    plan[6].append(functools.partial(diag_near, 2))
    plan[ACROSS].append(across_begin)
    plan[7].append(functools.partial(diag_near, 3))
    plan[12].append(functools.partial(across_near, 0))
    plan[14].append(functools.partial(across_near, 1))
    final = []
    for distance in range(1, grid_cols):
        for i in chunks:
            for k in range(PANELS):
                when = HOP + HOPS * (distance - 1) + (i - skip)
                (plan[when] if when < 4 * steps else final).append(functools.partial(panel_next, k, i, distance))
    for i in chunks:
        for k in range(PANELS):
            final.append(functools.partial(panel_arrived, k, i))

    def hook(b):
        def run(s):
            for t in range(steps):
                if plan[b * steps + t]:
                    @pl.when(s == t)
                    def _(t=t):
                        for action in plan[b * steps + t]:
                            action()
        return run

    diag[0, :half, half:] = jnp.zeros((half, width - half), jnp.float32)
    peers_entered(False)
    diag_out(ORDER[0])

    @pl.when(owner(me_row, me_col) & jnp.logical_not(owners[ORDER[0]]))
    def _():
        peers_entered(True)

    for p in ORDER[1:]:
        diag_out(p)

    @pl.when(jnp.logical_not(here_whole(0)))
    def _():
        mates_entered()

    diag_pass(0)
    for copy in share_copies:
        copy.start()
    diag_arrived(0)

    def inverted(b, value):
        aug[...] = value
        invert(aug, half, hook(b))
        return aug[...]

    def joined(k, first, second, below):
        inverse[k, :half, :half] = first
        inverse[k, :half, half:] = jnp.zeros((half, half), jnp.float32)
        inverse[k, half:, half:] = second
        inverse[k, half:, :half] = -update(second, update(below, first, 0), 0)

    inv0 = inverted(0, diag[0, :half, :half])
    inverse[0, :half, :half] = inv0
    diag_arrived(1)
    below0 = matmul_t(diag[0, half:, :half], inv0)
    cross[:half, :half] = below0
    inv1 = inverted(1, diag[0, half:, half:] - matmul_t(below0, below0))
    diag_arrived(2)
    below0, inv0 = cross[:half, :half], inverse[0, :half, :half]
    cross0 = matmul_t(diag[1, :, :half], inv0)
    cross1 = matmul_t(diag[1, :, half:] - matmul_t(cross0, below0), inv1)
    cross[:, :half] = cross0
    cross[:, half:] = cross1
    joined(0, inv0, inv1, below0)
    diag_arrived(3)
    rest[...] = diag[2] - matmul_t(cross0, cross0) - matmul_t(cross1, cross1)
    inv2 = inverted(2, rest[:half, :half])
    inverse[1, :half, :half] = inv2
    below1 = matmul_t(rest[half:, :half], inv2)
    left[0, :half, :half] = below1
    inv3 = inverted(3, rest[half:, half:] - matmul_t(below1, below1))
    joined(1, inverse[1, :half, :half], inv3, left[0, :half, :half])

    for action in final:
        action()
    kept = (row_blocks - skip) * rows_here
    left[0, : kept] = update(panel[0, skip:].reshape(kept, width), inverse[0], 1)
    left[1, : kept] = update(panel[1, skip:].reshape(kept, width) - update(left[0, :kept], cross[...], 1), inverse[1], 1)
    row = lax.broadcasted_iota(jnp.int32, (rows_here, width), 0) + me_layer * rows_here
    lower = row >= lax.broadcasted_iota(jnp.int32, (rows_here, width), 1)
    factor0 = jnp.where(lower, update(diag[0, here, :], inverse[0], 1), 0.0)
    factor1 = jnp.where(lower, update(rest[here, :], inverse[1], 1), 0.0)
    plain0 = cross[here, :] if skip else left[0, :rows_here]
    plain1 = factor1 if skip else left[1, :rows_here]
    first0 = jnp.where(me_row == 0, factor0, plain0)
    first1 = jnp.where(me_row == 0, 0.0, jnp.where(me_row == 1, factor1, plain1))

    def out_copy(slot):
        return [
            pltpu.make_async_copy(
                staged.at[slot, :, :, pl.ds(part * LANES, LANES)], out.at[:, :, slot * (width // LANES) + part, :], out_sem.at[slot, part]
            )
            for part in range(width // LANES)
        ]

    for slot in range(col_blocks):
        for k in range(PANELS):
            across_arrived(k, slot)
        share_copies[slot].wait()
        right0 = update(inverse[0], across[0, slot], 0)
        right1 = update(inverse[1], across[1, slot] - update(cross[...], right0, 0), 0)
        number = slot * grid_cols + me_col
        updated = share[slot, skip:].reshape(kept, width)
        updated -= update(left[0, :kept], right0, 0) + update(left[1, :kept], right1, 0)
        value = jnp.where(number == 0, left[0, :kept], jnp.where(number == 1, left[1, :kept], updated))
        staged[slot, skip:] = value.reshape(row_blocks - skip, rows_here, width)
        plain = 0.0 if skip else jnp.where(me_row < PANELS, 0.0, updated[:rows_here])
        staged[slot, 0] = jnp.where(number == 0, first0, jnp.where(number == 1, first1, plain))
        for copy in out_copy(slot):
            copy.start()

    for p in range(len(PIECES)):
        @pl.when(owners[p])
        def _(p=p):
            for col in range(grid_cols):
                if col == 0 and whole(p):
                    for _ in range(1, grid_rows):
                        wait(full(diag, p), diag_send.at[p, col])
                else:
                    wait(some(p, grid_rows if col else grid_rows - 1), diag_send.at[p, col])

        def sent(p=p):
            wait(some(p, len(targets(p))), pass_send.at[p])

        if whole(p):
            pl.when(jnp.logical_not(here_whole(p)))(sent)
        else:
            sent()
        if shared(p):
            wait(some(p, layers * split // pair), near_send.at[SHARED.index(p)])
    for k in range(PANELS):
        @pl.when(up(k))
        def _(k=k):
            wait(panel.at[k, skip:], panel_send.at[k, 1])

        if k:
            @pl.when(down(k))
            def _(k=k):
                wait(panel.at[k, skip:], panel_send.at[k, 0])

        @pl.when(me_row == k)
        def _(k=k):
            for slot in range(col_blocks):
                for n in range(1, grid_rows):
                    wait(across_half(k, slot), across_send.at[k, slot])
    if pair > 1:
        for k in range(PANELS):
            @pl.when(me_row != k)
            def _(k=k):
                for slot in range(col_blocks):
                    wait(across_half(k, slot), half_send.at[k, slot])
    for slot in range(col_blocks):
        for copy in out_copy(slot):
            copy.wait()


def keep(source, target, held, in_sem, out_sem):
    rows = source.shape[0] // KEEP
    parts = [pl.ds(n * rows, rows) for n in range(KEEP)]
    arrive = [pltpu.make_async_copy(source.at[part], held.at[part], in_sem.at[n]) for n, part in enumerate(parts)]
    leave = [pltpu.make_async_copy(held.at[part], target.at[part], out_sem.at[n]) for n, part in enumerate(parts)]
    for copy in arrive:
        copy.start()
    for n, copy in enumerate(leave):
        arrive[n].wait()
        copy.start()
    for copy in leave:
        copy.wait()


def local(sizes, schur_window):
    layers, grid_rows, grid_cols, row_blocks, col_blocks, width = sizes
    rows_here = width // layers
    anywhere = pl.BlockSpec(memory_space=pl.ANY)
    dma = pltpu.SemaphoreType.DMA
    pieces, diagonals, half = len(PIECES), len({p[2] for p in PIECES}), width // 2
    split = 2 if grid_rows % 2 == 0 else 1
    f32 = jnp.float32
    result = pl.pallas_call(
        functools.partial(kernel, sizes),
        out_shape=jax.ShapeDtypeStruct((row_blocks, rows_here, col_blocks * width // LANES, LANES), f32),
        in_specs=[anywhere],
        out_specs=anywhere,
        scratch_shapes=[
            pltpu.VMEM((diagonals, width, width), f32),
            pltpu.VMEM((PANELS, col_blocks, width, width), f32),
            pltpu.VMEM((PANELS, row_blocks, rows_here, width), f32),
            pltpu.VMEM((col_blocks, row_blocks, rows_here, width), f32),
            pltpu.VMEM((col_blocks, row_blocks, rows_here, width), f32),
            pltpu.VMEM((half, half), f32),
            pltpu.VMEM((PANELS, width, width), f32),
            pltpu.VMEM((width, width), f32),
            pltpu.VMEM((width, width), f32),
            pltpu.VMEM((PANELS, row_blocks * rows_here, width), f32),
            pltpu.SemaphoreType.REGULAR((grid_rows, grid_cols)),
            pltpu.SemaphoreType.REGULAR((layers, split)),
            dma((pieces, grid_cols)),
            dma((pieces,)),
            dma((pieces,)),
            dma((pieces,)),
            dma((len(SHARED),)),
            dma((len(SHARED),)),
            dma((PANELS, col_blocks)),
            dma((PANELS, col_blocks)),
            dma((PANELS, col_blocks)),
            dma((PANELS, col_blocks)),
            dma((PANELS, 2)),
            dma((PANELS, row_blocks)),
            dma((col_blocks,)),
            dma((col_blocks, width // LANES)),
        ],
        compiler_params=pltpu.CompilerParams(collective_id=0, has_side_effects=True),
        name="window",
    )(schur_window).reshape(-1, LANES)
    result = pl.pallas_call(
        keep, out_shape=jax.ShapeDtypeStruct(result.shape, f32), in_specs=[anywhere], out_specs=anywhere,
        scratch_shapes=[pltpu.VMEM(result.shape, f32), dma((KEEP,)), dma((KEEP,))], name="keep",
    )(result)
    return result.reshape(row_blocks, 1, rows_here, col_blocks, 1, width)


def solution(mesh):
    def body(schur_window):
        row_blocks, _, width, col_blocks, _, _ = schur_window.shape
        sizes = (mesh.shape["layer"], mesh.shape["row"], mesh.shape["col"], row_blocks, col_blocks, width)
        return local(sizes, schur_window)

    return jax.shard_map(
        body,
        mesh=mesh,
        in_specs=(P(None, "row", None, None, "col", None),),
        out_specs=P(None, "row", "layer", None, "col", None),
        check_vma=False,
    )
```
